32 devices in a mesh: ch: 4 (over z), ha: 2 (over x), dp: 4 (over y, core).
Axes of the slice: x: 2, y: 2, z: 4, core: 2. Of those that a mesh axis runs over, the one named last changes fastest.
Arguments:
- features: bfloat16 [384, 4, 4, 4, 128], P('ch', 'dp', None, 'ha'), may hold values from -26 to 26
- frame_count: int32 [4], P('dp'), may hold values from 1 to 4, as said below
- norm1_gain: float32 [384], P('ch'), may hold values from 0.5 to 2
- norm1_shift: float32 [384], P('ch'), may hold values from -3 to 3
- qkv_weight: bfloat16 [384, 1152], replicated, may hold values from -0.51031036 to 0.51031036
- qkv_bias: float32 [1152], replicated, may hold values from -3 to 3
- out_weight: bfloat16 [384, 384], replicated, may hold values from -0.3125 to 0.3125
- out_bias: float32 [384], replicated, may hold values from -3 to 3
- norm2_gain: float32 [384], P('ch'), may hold values from 0.5 to 2
- norm2_shift: float32 [384], P('ch'), may hold values from -3 to 3
- conv_weight: bfloat16 [3, 3, 3, 384, 384], P(None, None, None, 'ch'), may hold values from -0.0625 to 0.0625
- conv_bias: float32 [384], P('ch'), may hold values from -3 to 3
- cotangent: bfloat16 [384, 4, 4, 4, 128], P('ch', 'dp', None, 'ha'), may hold values from -0.0625 to 0.0625
Outputs:
- mixed: bfloat16 [384, 4, 4, 4, 128], P('ch', 'dp', None, 'ha')
- weight_grad: float32 [3, 3, 3, 384, 384], P(None, None, None, 'ch')
The draws below stay inside these ranges and needn't reach their ends.
Inputs may be any that keep to these rules, and one draw needn't show every extreme that they name: `frame_count`: some clip has all 4 frames valid and some clip only one.
All inputs are finite; a program needn't handle non-finite values.
Results may differ from the reference program's by a relative error of at most 0.015.
Values may be sent and summed in bfloat16 or wider, within the bound.
A program may use at most 64 MiB of HBM per device.

```python
import math
import jax
import jax.numpy as jnp
from jax import lax

C = 384
GROUPS = 32
FR = 4
W = 128
CLIPS = 4
HEIGHT = 4


def draw_features(key, part):
    first = jax.random.fold_in(jax.random.fold_in(key, 11), 0)
    shape = (C, CLIPS, FR, HEIGHT, W)
    height_pos = lax.broadcasted_iota(jnp.float32, shape, 3) / (HEIGHT - 1)
    ramp = 1.0 + 2.0 * height_pos
    return (jnp.clip(jax.random.normal(first, shape, jnp.float32), -5.0, 5.0) * ramp).astype(jnp.bfloat16)


def draw_frame_count(key, part):
    first, second = jax.random.split(jax.random.fold_in(key, 23))
    counts = jax.random.randint(first, (CLIPS,), 1, FR + 1)
    chosen = jax.random.randint(second, (), 0, CLIPS)
    other = (chosen + 1) % CLIPS
    places = jnp.arange(CLIPS)
    counts = jnp.where(places == chosen, FR, counts)
    counts = jnp.where(places == other, 1, counts)
    return counts.astype(jnp.int32)


def draw_qkv_weight(key, part):
    first, second, third = jax.random.split(jax.random.fold_in(key, 37), 3)
    query_w = jnp.clip(jax.random.normal(first, (C, C), jnp.float32), -5.0, 5.0) * (1.6 * C ** (-0.5))
    noise = jnp.clip(jax.random.normal(second, (C, C), jnp.float32), -5.0, 5.0)
    key_w = noise * (1.6 * C ** (-0.5))
    value_w = jnp.clip(jax.random.normal(third, (C, C), jnp.float32), -5.0, 5.0) * C ** (-0.5)
    return jnp.concatenate([query_w, key_w, value_w], axis=1).astype(jnp.bfloat16)


def shard_levels(rng, dims, pieces, least, largest):
    loudness, own = 1.0, jax.random.fold_in(rng, 6)
    for axis_at, blocks in pieces:
        draws = jnp.exp(jax.random.uniform(jax.random.fold_in(own, axis_at), (blocks,), jnp.float32, least / len(pieces), largest / len(pieces)))
        loudness = loudness * jnp.repeat(draws, dims[axis_at] // blocks).reshape([-1 if axis == axis_at else 1 for axis in range(len(dims))])
    return loudness


def gaussian(key, extent, width, most, cuts=(), dtype=jnp.bfloat16):
    drawn = jax.random.normal(key, extent, jnp.float32) * width
    if len(cuts) > 0:
        drawn = shard_levels(key, extent, cuts, -0.22, 0.18) * drawn
    return jnp.clip(drawn, min=-most, max=most).astype(dtype)


def setup_inputs(seed: int = 0) -> dict:
    seeds = jax.random.split(jax.random.key(seed), 14)
    features = draw_features(jax.random.fold_in(seeds[13], 71), 0)
    frame_count = draw_frame_count(jax.random.fold_in(seeds[13], 71), 0)
    norm1_gain = jnp.clip(jnp.exp(math.log(2.0) - 1.3862944 * jax.random.uniform(seeds[2], (C,), jnp.float32) ** shard_levels(seeds[2], (C,), ((0, 4),), -0.2, 0.2)), 0.5, 2.0)
    norm1_shift = gaussian(seeds[3], (C,), 0.5, 3.0, ((0, 4),), jnp.float32)
    qkv_weight = draw_qkv_weight(jax.random.fold_in(seeds[13], 71), 0)
    qkv_bias = gaussian(seeds[5], (3 * C,), 0.5, 3.0, (), jnp.float32)
    out_weight = gaussian(seeds[6], (C, C), C ** -0.5, 0.3125)
    out_bias = gaussian(seeds[7], (C,), 0.3, 3.0, (), jnp.float32)
    norm2_gain = jnp.clip(jnp.exp(math.log(2.0) - 1.3862944 * jax.random.uniform(seeds[8], (C,), jnp.float32) ** shard_levels(seeds[8], (C,), ((0, 4),), -0.2, 0.2)), 0.5, 2.0)
    norm2_shift = gaussian(seeds[9], (C,), 0.5, 3.0, ((0, 4),), jnp.float32)
    conv_weight = gaussian(seeds[10], (3, 3, 3, C, C), (27 * C) ** -0.5, 0.0625, ((3, 4),))
    conv_bias = gaussian(seeds[11], (C,), 0.3, 3.0, ((0, 4),), jnp.float32)
    cotangent = gaussian(seeds[12], (C, CLIPS, FR, HEIGHT, W), ((CLIPS * FR * HEIGHT * W) ** -0.5), 0.0625, ((0, 4), (1, 4), (3, 2)))
    return dict(features=features, frame_count=frame_count, norm1_gain=norm1_gain, norm1_shift=norm1_shift, qkv_weight=qkv_weight, qkv_bias=qkv_bias, out_weight=out_weight, out_bias=out_bias, norm2_gain=norm2_gain, norm2_shift=norm2_shift, conv_weight=conv_weight, conv_bias=conv_bias, cotangent=cotangent)


EPS = 1e-06

def frame_mask(frame_count):
    position = lax.broadcasted_iota(jnp.int32, (frame_count.shape[0], FR), 1)
    return (position < frame_count[:, None].astype(jnp.int32)).astype(jnp.float32)

def group_norm(values, mask, count, gain, shift):
    data = values.astype(jnp.float32).reshape(GROUPS, C // GROUPS, CLIPS, FR, HEIGHT * W)
    first = jnp.einsum('gkbfp,bf->gb', data, mask)
    second = jnp.einsum('gkbfp,bf->gb', data * data, mask)
    mean = first / count[None, :]
    var = second / count[None, :] - mean * mean
    scale = lax.rsqrt(var + EPS)
    normed = (data - mean[:, None, :, None, None]) * scale[:, None, :, None, None]
    normed = normed.reshape(C, CLIPS, FR, HEIGHT, W)
    return normed * gain[:, None, None, None, None] + shift[:, None, None, None, None]

def reference(features, frame_count, norm1_gain, norm1_shift, qkv_weight, qkv_bias, out_weight, out_bias, norm2_gain, norm2_shift, conv_weight, conv_bias, cotangent):
    mask = frame_mask(frame_count)
    count = frame_count.astype(jnp.float32) * (C // GROUPS * HEIGHT * W)
    normed = group_norm(features, mask, count, norm1_gain, norm1_shift).astype(jnp.bfloat16)
    frame_tokens = HEIGHT * W
    block_rows = math.gcd(frame_tokens, 1024)
    items = jnp.moveaxis(normed.reshape(C, CLIPS * FR, frame_tokens), 1, 0)
    qkv_full = qkv_weight.astype(jnp.float32)

    def attend_frame(item):
        proj = jnp.dot(item.T.astype(jnp.float32), qkv_full, preferred_element_type=jnp.float32) + qkv_bias
        proj = proj.astype(jnp.bfloat16)
        queries = proj[:, :C]
        keys = proj[:, C:2 * C].astype(jnp.float32)
        values = proj[:, 2 * C:].astype(jnp.float32)

        def one_block(query):
            scores = jnp.dot(query.astype(jnp.float32), keys.T, preferred_element_type=jnp.float32) * C ** (-0.5)
            top = lax.optimization_barrier(jnp.max(scores, axis=1, keepdims=True))
            weights = jnp.exp(scores - top)
            total = lax.optimization_barrier(jnp.sum(weights, axis=1, keepdims=True))
            rounded = lax.optimization_barrier(weights.astype(jnp.bfloat16))
            out = jnp.dot(rounded.astype(jnp.float32), values, preferred_element_type=jnp.float32) / total
            return out.astype(jnp.bfloat16)
        blocks = lax.map(one_block, queries.reshape(frame_tokens // block_rows, block_rows, C))
        return blocks.reshape(frame_tokens, C)
    attended = lax.map(attend_frame, items)
    update = lax.dot_general(out_weight.astype(jnp.float32), attended.astype(jnp.float32), (((0,), (2,)), ((), ())), preferred_element_type=jnp.float32)
    update = (update + out_bias[:, None, None]).astype(jnp.bfloat16).reshape(C, CLIPS, FR, HEIGHT, W)
    hidden = (features.astype(jnp.float32) + update.astype(jnp.float32)).astype(jnp.bfloat16)
    gated = jax.nn.silu(group_norm(hidden, mask, count, norm2_gain, norm2_shift)).astype(jnp.bfloat16)
    padded = jnp.pad(gated.astype(jnp.float32), ((0, 0), (0, 0), (2, 0), (1, 1), (1, 1)))
    masked_cot = (cotangent * mask.astype(jnp.bfloat16)[None, :, :, None, None]).astype(jnp.float32)
    conv = jnp.zeros((C, CLIPS, FR, HEIGHT, W), jnp.float32)
    grads = []
    for kt in range(3):
        for ky in range(3):
            for kx in range(3):
                window = padded[:, :, kt:kt + FR, ky:ky + HEIGHT, kx:kx + W]
                conv = conv + lax.dot_general(conv_weight[kt, ky, kx].astype(jnp.float32), window, (((0,), (0,)), ((), ())), preferred_element_type=jnp.float32)
                grads.append(lax.dot_general(window, masked_cot, (((1, 2, 3, 4), (1, 2, 3, 4)), ((), ())), preferred_element_type=jnp.float32))
    weight_grad = jnp.stack(grads).reshape(3, 3, 3, C, C)
    mixed = mask[None, :, :, None, None] * (hidden.astype(jnp.float32) + conv + conv_bias[:, None, None, None, None])
    return (mixed.astype(jnp.bfloat16), weight_grad)
```

```python
import functools

import jax
import jax.numpy as jnp
from jax import lax
from jax.experimental import pallas as pl
from jax.experimental.pallas import tpu as pltpu
from jax.sharding import PartitionSpec as P

GROUPS = 32


EPS = 1e-06


def padded_2(x, sides, width):
    for axis, dim in sides:
        count, length = (lax.axis_size(axis), x.shape[dim])
        up = [(i, (i + 1) % count) for i in range(count - 1)]
        down = [(j, i) for i, j in up]
        last = lax.slice_in_dim(x, length - width, length, axis=dim)
        leading = lax.slice_in_dim(x, 0, width, axis=dim)
        before = lax.ppermute(last, axis, up)
        after = lax.ppermute(leading, axis, down)
        x = jnp.concatenate([before, x, after], axis=dim)
    return x


def frame_mask(frame_count, frames):
    position = lax.broadcasted_iota(jnp.int32, (frame_count.shape[0], frames), 1)
    return (position < frame_count[:, None]).astype(jnp.float32)


def moments(values, mask, groups):
    chans, clips, frames, rows, cols = values.shape
    data = values.astype(jnp.float32).reshape(groups, chans // groups, clips, frames, rows * cols)
    first = jnp.einsum("gkbfp,bf->gb", data, mask)
    second = jnp.einsum("gkbfp,bf->gb", data * data, mask)
    return (first, second)


def normalize(values, first, second, count, gain, shift, groups):
    chans, clips, frames, rows, cols = values.shape
    mean = first / count[None, :]
    var = second / count[None, :] - mean * mean
    scale = lax.rsqrt(var + EPS)
    data = values.astype(jnp.float32).reshape(groups, chans // groups, clips, frames, rows * cols)
    normed = (data - mean[:, None, :, None, None]) * scale[:, None, :, None, None]
    normed = normed.reshape(values.shape)
    return normed * gain[:, None, None, None, None] + shift[:, None, None, None, None]


def attend(carry, queries, keys, values, scale):
    top, total, acc = carry
    scores = jnp.einsum("itc,isc->its", queries, keys, preferred_element_type=jnp.float32) * scale
    new_top = jnp.max(scores, axis=2)
    factor = jnp.exp(top - new_top)
    weights = jnp.exp(scores - new_top[..., None])
    total = total * factor + jnp.sum(weights, axis=2)
    acc = acc * factor[..., None] + jnp.einsum(
        "its,isc->itc", weights.astype(jnp.bfloat16), values, preferred_element_type=jnp.float32
    )
    return (new_top, total, acc)


def tap_stack(padded, time_tap, frames, rows, cols):
    windows = []
    for row_tap in range(3):
        for col_tap in range(3):
            windows.append(
                padded[
                    :,
                    :,
                    time_tap : time_tap + frames,
                    row_tap : row_tap + rows,
                    col_tap : col_tap + cols,
                ]
            )
    return jnp.concatenate(windows, axis=0)


def butterfly_sum(table, axes):
    steps = []
    for axis in axes:
        size = lax.axis_size(axis)
        for bit in range(size.bit_length() - 1):
            steps.append((axis, bit, size))
    length = table.shape[0]
    unit = (1 << len(steps)) * 8
    padded = -(-length // unit) * unit
    work = jnp.pad(table, ((0, padded - length), (0, 0)))
    for axis, bit, size in steps:
        side = (lax.axis_index(axis) >> bit) & 1
        halves = work.reshape(2, work.shape[0] // 2, work.shape[1])
        keep = lax.dynamic_index_in_dim(halves, side, keepdims=False)
        send = lax.dynamic_index_in_dim(halves, 1 - side, keepdims=False)
        perm = [(i, i ^ (1 << bit)) for i in range(size)]
        got = lax.ppermute(send.astype(jnp.bfloat16), axis, perm)
        work = keep + got.astype(jnp.float32)
    work = work.astype(jnp.bfloat16)
    for axis, bit, size in reversed(steps):
        side = (lax.axis_index(axis) >> bit) & 1
        perm = [(i, i ^ (1 << bit)) for i in range(size)]
        got = lax.ppermute(work, axis, perm)
        pair = jnp.stack([work, got])
        first = lax.dynamic_index_in_dim(pair, side, keepdims=False)
        second = lax.dynamic_index_in_dim(pair, 1 - side, keepdims=False)
        work = jnp.concatenate([first, second], axis=0)
    return work[:length].astype(jnp.float32)


def doubling_sum(values, axis):
    size = lax.axis_size(axis)
    for bit in range(size.bit_length() - 1):
        perm = [(i, i ^ (1 << bit)) for i in range(size)]
        got = lax.ppermute(values, axis, perm)
        values = tuple(a + b for a, b in zip(values, got))
    return values


def body(
    features,
    frame_count,
    norm1_gain,
    norm1_shift,
    qkv_weight,
    qkv_bias,
    out_weight,
    out_bias,
    norm2_gain,
    norm2_shift,
    conv_weight,
    conv_bias,
    cotangent,
):
    chans, clips, frames, rows, cols = features.shape
    groups = GROUPS // lax.axis_size("ch")
    mask = frame_mask(frame_count, frames)
    count = frame_count.astype(jnp.float32) * (chans // groups * rows * lax.axis_size("ha") * cols)
    first, second = moments(features, mask, groups)
    first, second = doubling_sum((first, second), "ha")
    normed = normalize(features, first, second, count, norm1_gain, norm1_shift, groups).astype(
        jnp.bfloat16
    )
    by_frame = lax.all_to_all(normed, "ch", split_axis=2, concat_axis=0, tiled=True)
    width = by_frame.shape[0]
    items = clips * by_frame.shape[2]
    tok_rows = rows * cols
    tokens = by_frame.reshape(width, items, tok_rows)
    queries = lax.dot_general(
        tokens, qkv_weight[:, :width], (((0,), (0,)), ((), ())), preferred_element_type=jnp.float32
    )
    queries = (queries + qkv_bias[:width]).astype(jnp.bfloat16)
    scale = width ** (-0.5)
    start_carry = (
        jnp.full((items, tok_rows), -jnp.inf, jnp.float32),
        jnp.zeros((items, tok_rows), jnp.float32),
        jnp.zeros((items, tok_rows, width), jnp.float32),
    )
    pairs = lax.dot_general(
        tokens, qkv_weight[:, width:], (((0,), (0,)), ((), ())), preferred_element_type=jnp.float32
    )
    pairs = (pairs + qkv_bias[width:]).astype(jnp.bfloat16)
    piece = lax.all_gather(pairs, "ha", axis=1, tiled=True)
    top, total, acc = attend(start_carry, queries, piece[..., :width], piece[..., width:], scale)
    attended = (acc / total[..., None]).astype(jnp.bfloat16)
    projected = lax.dot_general(
        out_weight, attended, (((0,), (2,)), ((), ())), preferred_element_type=jnp.float32
    )
    projected = (projected + out_bias[:, None, None]).astype(jnp.bfloat16).reshape(by_frame.shape)
    update = lax.all_to_all(projected, "ch", split_axis=0, concat_axis=2, tiled=True)
    hidden = (features.astype(jnp.float32) + update.astype(jnp.float32)).astype(jnp.bfloat16)
    first, second = moments(hidden, mask, groups)
    first, second = doubling_sum((first, second), "ha")
    gated = jax.nn.silu(
        normalize(hidden, first, second, count, norm2_gain, norm2_shift, groups)
    ).astype(jnp.bfloat16)
    with_rows = padded_2(gated, (("ha", 3),), 1)
    padded = jnp.pad(with_rows, ((0, 0), (0, 0), (2, 0), (0, 0), (1, 1)))
    stacks = [tap_stack(padded, time_tap, frames, rows, cols) for time_tap in range(3)]
    amount = chans * lax.axis_size("ch")
    summed = jnp.zeros((amount, clips, frames, rows, cols), jnp.float32)
    for time_tap in range(3):
        part = conv_weight[time_tap].reshape(9 * chans, amount)
        summed = summed + lax.dot_general(
            part, stacks[time_tap], (((0,), (0,)), ((), ())), preferred_element_type=jnp.float32
        )
    summed, stacks = lax.optimization_barrier((summed.astype(jnp.bfloat16), stacks))
    shares = lax.axis_size("ch")
    parts = summed.reshape((shares, amount // shares) + summed.shape[1:])
    parts = lax.all_to_all(parts, "ch", split_axis=0, concat_axis=0, tiled=True)
    conv_out = jnp.sum(parts.astype(jnp.float32), axis=0)
    mixed = mask[None, :, :, None, None] * (
        hidden.astype(jnp.float32) + conv_out + conv_bias[:, None, None, None, None]
    )
    mixed = mixed.astype(jnp.bfloat16)
    masked_cot = cotangent * mask.astype(jnp.bfloat16)[None, :, :, None, None]
    full_width = chans * lax.axis_size("ch")
    carry = jnp.zeros((3, 9 * chans, full_width), jnp.float32)
    copies = jnp.broadcast_to(masked_cot[None], (shares,) + masked_cot.shape)
    piece = lax.all_to_all(copies, "ch", split_axis=0, concat_axis=0, tiled=True)
    piece = piece.reshape((shares * chans,) + masked_cot.shape[1:])
    start = jnp.int32(0)
    for time_tap in range(3):
        part = lax.dot_general(
            stacks[time_tap],
            piece,
            (((1, 2, 3, 4), (1, 2, 3, 4)), ((), ())),
            preferred_element_type=jnp.float32,
        )
        carry = lax.dynamic_update_slice(
            carry, part[None], (jnp.int32(time_tap), jnp.int32(0), start)
        )
    weight_grad = butterfly_sum(carry.reshape(27 * chans, full_width), ("dp", "ha"))
    weight_grad = weight_grad.reshape(3, 3, 3, chans, full_width)
    return (mixed, weight_grad)


MESH = pl.DeviceIdType.MESH
HIGH = lax.Precision.HIGHEST
SEMS = 96
TAPS = 27
PER_CHUNK = 4
CHUNKS = 7


def fits_fused(mesh):
    return mesh.shape["ch"] == 4 and mesh.shape["ha"] == 2 and mesh.shape["dp"] == 4


def nt_dot(a, b, precision=None):
    return lax.dot_general(
        a, b, (((1,), (1,)), ((), ())), preferred_element_type=jnp.float32, precision=precision
    )


def nn_dot(a, b, precision=None):
    return lax.dot_general(
        a, b, (((1,), (0,)), ((), ())), preferred_element_type=jnp.float32, precision=precision
    )


def column_of(row):
    parts = []
    for k in range(row.shape[1] // 128):
        block = jnp.broadcast_to(row[:, k * 128 : (k + 1) * 128], (128, 128))
        parts.append(block.T)
    return parts[0] if len(parts) == 1 else jnp.concatenate(parts, axis=0)


def wide(column):
    return jnp.concatenate([column, column], axis=1)


def group_sums(blocks, masks, groups):
    chans = blocks[0].shape[0]
    first = second = None
    for block, keep in zip(blocks, masks):
        one = block[:, :128] + block[:, 128:]
        sq = block * block
        two = sq[:, :128] + sq[:, 128:]
        first = one * keep if first is None else first + one * keep
        second = two * keep if second is None else second + two * keep
    ones = jnp.ones((8, 128), jnp.float32)
    size = chans // groups
    row = lax.broadcasted_iota(jnp.int32, (chans, 128), 0)
    lane = lax.broadcasted_iota(jnp.int32, (chans, 128), 1)
    row_group = jnp.zeros((chans, 128), jnp.int32)
    lane_group = jnp.zeros((chans, 128), jnp.int32)
    for g in range(1, groups):
        row_group = row_group + (row >= g * size).astype(jnp.int32)
        lane_group = lane_group + (lane >= g * size).astype(jnp.int32)
    same = ((row_group == lane_group) & (lane < chans)).astype(jnp.float32)
    sums = nt_dot(ones, first, HIGH)
    squares = nt_dot(ones, second, HIGH)
    return nn_dot(sums, same, HIGH), nn_dot(squares, same, HIGH)


def fused_kernel(
    groups,
    all_rows,
    fc_ref,
    feat_ref,
    cot_ref,
    n1g_ref,
    n1s_ref,
    n2g_ref,
    n2s_ref,
    cb_ref,
    qkvb_ref,
    ob_ref,
    wq_any,
    wo_any,
    wc_any,
    mixed_ref,
    res_ref,
    wq_ref,
    wo_ref,
    wc_ref,
    wqt_ref,
    wot_ref,
    wct_ref,
    qkvb_col,
    ob_col,
    cb_col,
    stat_ref,
    raw_ref,
    nrm_ref,
    qkv_ref,
    upd_s,
    upd_r,
    stat2_ref,
    halo_s,
    halo_r,
    hid_ref,
    gate_ref,
    stack_ref,
    cot_all,
    conv_s,
    conv_r,
    part_ref,
    s1,
    r1,
    s2,
    r2,
    s3,
    r3,
    send_sem,
    recv_sem,
    local_sem,
):
    frames, chans, span = feat_ref.shape
    nch = 4
    full = nch * chans
    z = lax.axis_index("ch")
    x = lax.axis_index("ha")
    d = lax.axis_index("dp")
    core = lax.rem(d, 2)
    yy = lax.div(d, 2)
    core_peer = {"dp": d + 1 - 2 * core}
    y_peer = {"dp": lax.rem(d + 2, 4)}
    x_peer = {"ha": 1 - x}
    count_f = fc_ref[0]
    masks = [jnp.where(f < count_f, 1.0, 0.0).astype(jnp.float32) for f in range(frames)]

    counter = [0]
    pending = []

    def copy_to(src, dst, dev, start=True):
        k = counter[0]
        counter[0] += 1
        c = pltpu.make_async_remote_copy(
            src_ref=src,
            dst_ref=dst,
            send_sem=send_sem.at[k],
            recv_sem=recv_sem.at[k],
            device_id=dev,
            device_id_type=MESH,
        )
        if start:
            c.start()
            pending.append(c)
        return c, k

    def arrived(dst, k):
        pltpu.make_async_remote_copy(
            src_ref=dst,
            dst_ref=dst,
            send_sem=send_sem.at[k],
            recv_sem=recv_sem.at[k],
            device_id=x_peer,
            device_id_type=MESH,
        ).wait_recv()

    loads = []
    for k, (a, b) in enumerate(((wq_any, wq_ref), (wo_any, wo_ref), (wc_any, wc_ref))):
        c = pltpu.make_async_copy(a, b, local_sem.at[k])
        c.start()
        loads.append(c)

    barrier = pltpu.get_barrier_semaphore()
    ahead = [lax.rem(z + j, nch) for j in range(nch)]
    behind = [lax.rem(z + nch - j, nch) for j in range(nch)]
    partners = [core_peer, y_peer, x_peer]
    for j in range(1, nch):
        partners.append({"ch": ahead[j]})
        partners.append({"ch": ahead[j], "ha": 1 - x})
    for dev in partners:
        pl.semaphore_signal(barrier, inc=1, device_id=dev, device_id_type=MESH)

    first, second = group_sums(
        [feat_ref[f].astype(jnp.float32) for f in range(frames)], masks, groups
    )
    lanes_pad = jnp.zeros((1, 128 - chans), jnp.float32)
    own = stat_ref.at[0, z]
    own[...] = jnp.zeros((8, 128), jnp.float32)
    own[0:1, :] = first[0:1, :]
    own[1:2, :] = second[0:1, :]
    own[2:3, :] = jnp.concatenate([n1g_ref[...], lanes_pad], axis=1)
    own[3:4, :] = jnp.concatenate([n1s_ref[...], lanes_pad], axis=1)

    pl.semaphore_wait(barrier, len(partners))

    feat_k = {}
    for j in range(1, nch):
        _, feat_k[j] = copy_to(feat_ref.at[ahead[j]], raw_ref.at[0, z], {"ch": ahead[j]})
    _, feat_own_k = copy_to(feat_ref.at[z], raw_ref.at[1, z], x_peer)
    stat_k = []
    for j in range(nch):
        if j:
            _, k = copy_to(stat_ref.at[0, z], stat_ref.at[0, z], {"ch": ahead[j]})
            stat_k.append((0, j, k))
        _, k = copy_to(stat_ref.at[0, z], stat_ref.at[1, z], {"ch": ahead[j], "ha": 1 - x})
        stat_k.append((1, j, k))
    raw_ref[0, z] = feat_ref[z]

    qkvb_col[...] = column_of(qkvb_ref[...])
    ob_col[...] = column_of(ob_ref[...])
    cb_col[...] = column_of(jnp.concatenate([cb_ref[...], lanes_pad], axis=1))[:chans]
    stack_ref[:, 0 : 2 * span] = jnp.zeros((9 * chans, 2 * span), jnp.bfloat16)
    own_rows = pl.ds(pl.multiple_of(z * chans, chans), chans)
    for f in range(frames):
        cot_all[own_rows, f * span : (f + 1) * span] = (
            cot_ref[f].astype(jnp.float32) * masks[f]
        ).astype(jnp.bfloat16)
    loads[0].wait()
    for k in range(9):
        wqt_ref[k * 128 : (k + 1) * 128, :] = wq_ref[:, k * 128 : (k + 1) * 128].T
    loads[1].wait()
    for k in range(3):
        wot_ref[k * 128 : (k + 1) * 128, :] = wo_ref[:, k * 128 : (k + 1) * 128].T

    fwd_k = {}
    for j in range(1, nch):
        zs = behind[j]
        arrived(raw_ref.at[0, zs], feat_k[j])
        _, fwd_k[j] = copy_to(raw_ref.at[0, zs], raw_ref.at[1, zs], x_peer)

    line_k = {}

    def line_step(step):
        up, ku = copy_to(
            cot_all.at[pl.ds(pl.multiple_of((z - step + 1) * chans, chans), chans)],
            cot_all.at[pl.ds(pl.multiple_of((z - step + 1) * chans, chans), chans)],
            {"ch": lax.rem(z + 1, nch)},
            start=False,
        )
        down, kd = copy_to(
            cot_all.at[pl.ds(pl.multiple_of((z + step - 1) * chans, chans), chans)],
            cot_all.at[pl.ds(pl.multiple_of((z + step - 1) * chans, chans), chans)],
            {"ch": lax.rem(z + nch - 1, nch)},
            start=False,
        )
        line_k[step] = (up, ku, down, kd)

        @pl.when((z - step + 1 >= 0) & (z + 1 < nch))
        def _():
            up.start()

        @pl.when((z + step - 1 < nch) & (z >= 1))
        def _():
            down.start()

    def line_wait(step):
        _, ku, _, kd = line_k[step]

        @pl.when(z - step >= 0)
        def _():
            arrived(cot_all.at[pl.ds(pl.multiple_of((z - step) * chans, chans), chans)], ku)

        @pl.when(z + step < nch)
        def _():
            arrived(cot_all.at[pl.ds(pl.multiple_of((z + step) * chans, chans), chans)], kd)

    def line_finish(step):
        up, _, down, _ = line_k[step]

        @pl.when((z - step + 1 >= 0) & (z + 1 < nch))
        def _():
            up.wait_send()

        @pl.when((z + step - 1 < nch) & (z >= 1))
        def _():
            down.wait_send()

    line_step(1)

    for side, j, k in stat_k:
        arrived(stat_ref.at[side, behind[j]], k)
    entries = count_f.astype(jnp.float32) * float(chans // groups * all_rows * 128)

    def norm_columns(total, total_sq, gain, shift):
        mean = total / entries
        var = total_sq / entries - mean * mean
        scale = lax.rsqrt(var + EPS) * gain
        return [wide(column_of(v)[:chans]) for v in (mean, scale, shift)]

    cols = []
    for c in range(nch):
        both = stat_ref[0, c] + stat_ref[1, c]
        cols.append(
            norm_columns(both[0:1], both[1:2], stat_ref[0, c, 2:3], stat_ref[0, c, 3:4])
        )

    def normalize_side(side):
        for c in range(nch):
            mean, scale, shift = cols[c]
            block = raw_ref[side, c].astype(jnp.float32)
            nrm_ref[c * chans : (c + 1) * chans, side * span : (side + 1) * span] = (
                (block - mean) * scale + shift
            ).astype(jnp.bfloat16)

    normalize_side(0)
    bias = wide(qkvb_col[...])
    qkv_ref[:, 0:span] = (nn_dot(wqt_ref[...], nrm_ref[:, 0:span]) + bias).astype(jnp.bfloat16)
    arrived(raw_ref.at[1, z], feat_own_k)
    for j in range(1, nch):
        arrived(raw_ref.at[1, behind[j]], fwd_k[j])
    normalize_side(1)
    qkv_ref[full:, span:] = (
        nn_dot(wqt_ref[full:, :], nrm_ref[:, span:]) + bias[full:]
    ).astype(jnp.bfloat16)

    keys = qkv_ref[full : 2 * full, :].T
    scores = nn_dot(keys, qkv_ref[0:full, 0:span]) * (full ** (-0.5))
    top = jnp.max(scores, axis=0, keepdims=True)
    weights = jnp.exp(scores - top)
    total = jnp.sum(weights, axis=0, keepdims=True)
    attended = nn_dot(qkv_ref[2 * full :, :], weights.astype(jnp.bfloat16)) / total
    update = nn_dot(wot_ref[...], attended.astype(jnp.bfloat16)) + wide(ob_col[...])
    update = update.astype(jnp.bfloat16)
    for c in range(nch):
        upd_s[c] = update[c * chans : (c + 1) * chans]
    upd_k = {}
    for j in range(1, nch):
        _, upd_k[j] = copy_to(upd_s.at[ahead[j]], upd_r.at[z], {"ch": ahead[j]})
    upd_r[z] = upd_s[z]

    loads[2].wait()
    for k in range(TAPS * chans // 96):
        wct_ref[:, k * 96 : (k + 1) * 96] = wc_ref[k * 96 : (k + 1) * 96, :].T

    line_wait(1)
    for j in range(1, nch):
        arrived(upd_r.at[behind[j]], upd_k[j])
    line_step(2)

    hidden = []
    for f in range(frames):
        h = (feat_ref[f].astype(jnp.float32) + upd_r[f].astype(jnp.float32)).astype(jnp.bfloat16)
        hid_ref[f] = h
        hidden.append(h.astype(jnp.float32))
        halo_s[f] = jnp.where(x == 0, h[:, 128:], h[:, :128])
    _, halo_k = copy_to(halo_s, halo_r, x_peer)
    first, second = group_sums(hidden, masks, groups)
    stat2_ref[0] = jnp.zeros((8, 128), jnp.float32)
    stat2_ref[0, 0:1, :] = first[0:1, :]
    stat2_ref[0, 1:2, :] = second[0:1, :]
    _, stat2_k = copy_to(stat2_ref.at[0], stat2_ref.at[1], x_peer)
    arrived(stat2_ref.at[1], stat2_k)
    both = stat2_ref[0] + stat2_ref[1]
    gain2 = jnp.concatenate([n2g_ref[...], lanes_pad], axis=1)
    shift2 = jnp.concatenate([n2s_ref[...], lanes_pad], axis=1)
    mean2, scale2, shift2 = norm_columns(both[0:1], both[1:2], gain2, shift2)
    mean2, scale2, shift2 = mean2[:, :128], scale2[:, :128], shift2[:, :128]
    lane = lax.broadcasted_iota(jnp.int32, (chans, 128), 1)

    def place(f, row, values):
        left = jnp.where(lane == 0, 0.0, pltpu.roll(values, 1, 1)).astype(jnp.bfloat16)
        right = jnp.where(lane == 127, 0.0, pltpu.roll(values, 127, 1)).astype(jnp.bfloat16)
        centre = values.astype(jnp.bfloat16)
        for row_tap in range(3):
            out_row = row + 1 - row_tap
            if out_row < 0 or out_row > 1:
                continue
            at = (f + 2) * span + out_row * 128
            for col_tap, v in enumerate((left, centre, right)):
                tap = row_tap * 3 + col_tap
                stack_ref[tap * chans : (tap + 1) * chans, at : at + 128] = v

    def gate(values):
        u = (values - mean2) * scale2 + shift2
        return u / (1.0 + jnp.exp(-u))

    for f in range(frames):
        for r in range(2):
            values = gate(hid_ref[f, :, r * 128 : (r + 1) * 128].astype(jnp.float32))
            place(f, r, values)
    arrived(halo_r, halo_k)
    for f in range(frames):
        values = gate(halo_r[f].astype(jnp.float32))
        place(f, -1, jnp.where(x == 1, values, 0.0))
        place(f, 2, jnp.where(x == 0, values, 0.0))

    line_wait(2)
    line_step(3)

    conv_k = {}

    def conv_frame(f):
        acc = None
        for kt in range(3):
            term = nn_dot(
                wct_ref[:, kt * 9 * chans : (kt + 1) * 9 * chans],
                stack_ref[:, (f + kt) * span : (f + kt + 1) * span],
            )
            acc = term if acc is None else acc + term
        acc = acc.astype(jnp.bfloat16)
        for c in range(nch):
            conv_s[f, c] = acc[c * chans : (c + 1) * chans]
        for j in range(1, nch):
            _, conv_k[f, j] = copy_to(
                conv_s.at[f, ahead[j]], conv_r.at[f, z], {"ch": ahead[j]}
            )

    part_ref[TAPS] = jnp.zeros((chans, full), jnp.float32)

    def grad_chunk(c):
        tap = PER_CHUNK * c
        while tap < min(PER_CHUNK * (c + 1), TAPS):
            kt = tap // 9
            stop = min(PER_CHUNK * (c + 1), 9 * (kt + 1), TAPS)
            lo, hi = tap - 9 * kt, stop - 9 * kt
            value = nt_dot(
                stack_ref[lo * chans : hi * chans, kt * span : kt * span + frames * span],
                cot_all[...],
            )
            for k in range(stop - tap):
                part_ref[tap + k] = value[k * chans : (k + 1) * chans]
            tap = stop

    half = PER_CHUNK // 2
    keys_of = [dict() for _ in range(CHUNKS)]
    quarter = chans // 2

    def axes_of(c):
        if c % 2 == 0:
            return (x, x_peer), (yy, y_peer)
        return (yy, y_peer), (x, x_peer)

    def stage1(c):
        for k in range(half):
            s1[c, k] = part_ref[PER_CHUNK * c + half * (1 - core) + k].astype(jnp.bfloat16)
        _, keys_of[c][1] = copy_to(s1.at[c], r1.at[c], core_peer)

    def own_tap(c, k):
        return PER_CHUNK * c + half * core + k

    def stage2(c):
        (a, a_peer), _ = axes_of(c)
        arrived(r1.at[c], keys_of[c][1])
        give = 1 - a
        s2[c] = (part_ref[own_tap(c, give)] + r1[c, give].astype(jnp.float32)).astype(jnp.bfloat16)
        _, keys_of[c][2] = copy_to(s2.at[c], r2.at[c], a_peer)
        part_ref[own_tap(c, a)] = part_ref[own_tap(c, a)] + r1[c, a].astype(jnp.float32)

    def rows_of(b):
        return pl.ds(pl.multiple_of(b * quarter, quarter), quarter)

    def stage3(c):
        (a, _), (b, b_peer) = axes_of(c)
        arrived(r2.at[c], keys_of[c][2])
        t = own_tap(c, a)
        s3[c] = (
            part_ref[t, rows_of(1 - b)] + r2[c, rows_of(1 - b)].astype(jnp.float32)
        ).astype(jnp.bfloat16)
        _, keys_of[c][3] = copy_to(s3.at[c], r3.at[c], b_peer)
        part_ref[t, rows_of(b)] = part_ref[t, rows_of(b)] + r2[c, rows_of(b)].astype(jnp.float32)

    def stage4(c):
        (a, _), (b, b_peer) = axes_of(c)
        arrived(r3.at[c], keys_of[c][3])
        t = own_tap(c, a)
        res_ref[t, rows_of(b)] = (part_ref[t, rows_of(b)] + r3[c].astype(jnp.float32)).astype(
            jnp.bfloat16
        )
        _, keys_of[c][4] = copy_to(res_ref.at[t, rows_of(b)], res_ref.at[t, rows_of(b)], b_peer)

    def stage5(c):
        (a, a_peer), (b, _) = axes_of(c)
        t = own_tap(c, a)
        arrived(res_ref.at[t, rows_of(1 - b)], keys_of[c][4])
        _, keys_of[c][5] = copy_to(res_ref.at[t], res_ref.at[t], a_peer)

    def stage6(c):
        (a, _), _ = axes_of(c)
        arrived(res_ref.at[own_tap(c, 1 - a)], keys_of[c][5])
        pair = pl.ds(PER_CHUNK * c + half * core, half)
        _, keys_of[c][6] = copy_to(res_ref.at[pair], res_ref.at[pair], core_peer)

    def stage7(c):
        arrived(res_ref.at[pl.ds(PER_CHUNK * c + half * (1 - core), half)], keys_of[c][6])

    stages = [None, stage1, stage2, stage3, stage4, stage5, stage6, stage7]

    line_wait(3)
    for step in range(CHUNKS + 7):
        if step < CHUNKS:
            grad_chunk(step)
            stage1(step)
        if 2 <= step < 2 + frames:
            conv_frame(step - 2)
        for s in range(2, 8):
            c = step - (s - 1)
            if 0 <= c < CHUNKS:
                stages[s](c)

    conv_bias = wide(cb_col[...])
    for f in range(frames):
        total = hid_ref[f].astype(jnp.float32) + conv_bias
        for j in range(1, nch):
            arrived(conv_r.at[f, behind[j]], conv_k[f, j])
        total = total + conv_s[f, z].astype(jnp.float32)
        for j in range(1, nch):
            total = total + conv_r[f, behind[j]].astype(jnp.float32)
        mixed_ref[f] = (total * masks[f]).astype(jnp.bfloat16)

    for c in pending:
        c.wait_send()
    for step in (1, 2, 3):
        line_finish(step)


def fused_body(
    features,
    frame_count,
    norm1_gain,
    norm1_shift,
    qkv_weight,
    qkv_bias,
    out_weight,
    out_bias,
    norm2_gain,
    norm2_shift,
    conv_weight,
    conv_bias,
    cotangent,
):
    chans, clips, frames, rows, cols = features.shape
    nch = lax.axis_size("ch")
    full = nch * chans
    span = rows * cols
    groups = GROUPS // nch

    def by_frame(v):
        return jnp.transpose(v.reshape(chans, frames, span), (1, 0, 2))

    bf16, f32 = jnp.bfloat16, jnp.float32
    vm = pltpu.VMEM
    vmem = pl.BlockSpec(memory_space=pltpu.VMEM)
    anyspace = pl.BlockSpec(memory_space=pl.ANY)
    scratch = [
        vm((full, 3 * full), bf16),
        vm((full, full), bf16),
        vm((TAPS * chans, full), bf16),
        vm((3 * full, full), bf16),
        vm((full, full), bf16),
        vm((full, TAPS * chans), bf16),
        vm((3 * full, 128), f32),
        vm((full, 128), f32),
        vm((chans, 128), f32),
        vm((2, nch, 8, 128), f32),
        vm((2, nch, chans, span), bf16),
        vm((full, 2 * span), bf16),
        vm((3 * full, 2 * span), bf16),
        vm((nch, chans, span), bf16),
        vm((nch, chans, span), bf16),
        vm((2, 8, 128), f32),
        vm((frames, chans, 128), bf16),
        vm((frames, chans, 128), bf16),
        vm((frames, chans, span), bf16),
        vm((8, 128), f32),
        vm((9 * chans, (frames + 2) * span), bf16),
        vm((full, frames * span), bf16),
        vm((frames, nch, chans, span), bf16),
        vm((frames, nch, chans, span), bf16),
        vm((TAPS + 1, chans, full), f32),
        vm((CHUNKS, 2, chans, full), bf16),
        vm((CHUNKS, 2, chans, full), bf16),
        vm((CHUNKS, chans, full), bf16),
        vm((CHUNKS, chans, full), bf16),
        vm((CHUNKS, chans // 2, full), bf16),
        vm((CHUNKS, chans // 2, full), bf16),
        pltpu.SemaphoreType.DMA((SEMS,)),
        pltpu.SemaphoreType.DMA((SEMS,)),
        pltpu.SemaphoreType.DMA((3,)),
    ]
    mixed, grad = pl.pallas_call(
        functools.partial(fused_kernel, groups, rows * lax.axis_size("ha")),
        out_shape=(
            jax.ShapeDtypeStruct((frames, chans, span), bf16),
            jax.ShapeDtypeStruct((TAPS + 1, chans, full), bf16),
        ),
        in_specs=[pl.BlockSpec(memory_space=pltpu.SMEM)] + [vmem] * 9 + [anyspace] * 3,
        out_specs=(vmem, vmem),
        scratch_shapes=scratch,
        compiler_params=pltpu.CompilerParams(
            collective_id=0, has_side_effects=True, vmem_limit_bytes=48 * 1024 * 1024
        ),
    )(
        frame_count,
        by_frame(features),
        by_frame(cotangent),
        norm1_gain.reshape(1, chans),
        norm1_shift.reshape(1, chans),
        norm2_gain.reshape(1, chans),
        norm2_shift.reshape(1, chans),
        conv_bias.reshape(1, chans),
        qkv_bias.reshape(1, 3 * full),
        out_bias.reshape(1, full),
        qkv_weight,
        out_weight,
        conv_weight.reshape(TAPS * chans, full),
    )
    mixed = jnp.transpose(mixed, (1, 0, 2)).reshape(chans, clips, frames, rows, cols)
    grad = grad[:TAPS].astype(f32).reshape(3, 3, 3, chans, full)
    return mixed, grad


def solution(mesh):
    placed = (
        P("ch", "dp", None, "ha", None),
        P("dp"),
        P("ch"),
        P("ch"),
        P(),
        P(),
        P(),
        P(),
        P("ch"),
        P("ch"),
        P(None, None, None, "ch", None),
        P("ch"),
        P("ch", "dp", None, "ha", None),
    )
    return jax.shard_map(
        fused_body if fits_fused(mesh) else body,
        mesh=mesh,
        in_specs=placed,
        out_specs=(P("ch", "dp", None, "ha", None), P(None, None, None, "ch", None)),
        check_vma=False,
    )
```

```python
import functools

import jax
import jax.numpy as jnp
from jax import lax
from jax.experimental import pallas as pl
from jax.experimental.pallas import tpu as pltpu
from jax.sharding import PartitionSpec as P

GROUPS = 32


EPS = 1e-06


def padded_2(x, sides, width):
    for axis, dim in sides:
        count, length = (lax.axis_size(axis), x.shape[dim])
        up = [(i, (i + 1) % count) for i in range(count - 1)]
        down = [(j, i) for i, j in up]
        last = lax.slice_in_dim(x, length - width, length, axis=dim)
        leading = lax.slice_in_dim(x, 0, width, axis=dim)
        before = lax.ppermute(last, axis, up)
        after = lax.ppermute(leading, axis, down)
        x = jnp.concatenate([before, x, after], axis=dim)
    return x


def frame_mask(frame_count, frames):
    position = lax.broadcasted_iota(jnp.int32, (frame_count.shape[0], frames), 1)
    return (position < frame_count[:, None]).astype(jnp.float32)


def moments(values, mask, groups):
    chans, clips, frames, rows, cols = values.shape
    data = values.astype(jnp.float32).reshape(groups, chans // groups, clips, frames, rows * cols)
    first = jnp.einsum("gkbfp,bf->gb", data, mask)
    second = jnp.einsum("gkbfp,bf->gb", data * data, mask)
    return (first, second)


def normalize(values, first, second, count, gain, shift, groups):
    chans, clips, frames, rows, cols = values.shape
    mean = first / count[None, :]
    var = second / count[None, :] - mean * mean
    scale = lax.rsqrt(var + EPS)
    data = values.astype(jnp.float32).reshape(groups, chans // groups, clips, frames, rows * cols)
    normed = (data - mean[:, None, :, None, None]) * scale[:, None, :, None, None]
    normed = normed.reshape(values.shape)
    return normed * gain[:, None, None, None, None] + shift[:, None, None, None, None]


def attend(carry, queries, keys, values, scale):
    top, total, acc = carry
    scores = jnp.einsum("itc,isc->its", queries, keys, preferred_element_type=jnp.float32) * scale
    new_top = jnp.max(scores, axis=2)
    factor = jnp.exp(top - new_top)
    weights = jnp.exp(scores - new_top[..., None])
    total = total * factor + jnp.sum(weights, axis=2)
    acc = acc * factor[..., None] + jnp.einsum(
        "its,isc->itc", weights.astype(jnp.bfloat16), values, preferred_element_type=jnp.float32
    )
    return (new_top, total, acc)


def tap_stack(padded, time_tap, frames, rows, cols):
    windows = []
    for row_tap in range(3):
        for col_tap in range(3):
            windows.append(
                padded[
                    :,
                    :,
                    time_tap : time_tap + frames,
                    row_tap : row_tap + rows,
                    col_tap : col_tap + cols,
                ]
            )
    return jnp.concatenate(windows, axis=0)


def butterfly_sum(table, axes):
    steps = []
    for axis in axes:
        size = lax.axis_size(axis)
        for bit in range(size.bit_length() - 1):
            steps.append((axis, bit, size))
    length = table.shape[0]
    unit = (1 << len(steps)) * 8
    padded = -(-length // unit) * unit
    work = jnp.pad(table, ((0, padded - length), (0, 0)))
    for axis, bit, size in steps:
        side = (lax.axis_index(axis) >> bit) & 1
        halves = work.reshape(2, work.shape[0] // 2, work.shape[1])
        keep = lax.dynamic_index_in_dim(halves, side, keepdims=False)
        send = lax.dynamic_index_in_dim(halves, 1 - side, keepdims=False)
        perm = [(i, i ^ (1 << bit)) for i in range(size)]
        got = lax.ppermute(send.astype(jnp.bfloat16), axis, perm)
        work = keep + got.astype(jnp.float32)
    work = work.astype(jnp.bfloat16)
    for axis, bit, size in reversed(steps):
        side = (lax.axis_index(axis) >> bit) & 1
        perm = [(i, i ^ (1 << bit)) for i in range(size)]
        got = lax.ppermute(work, axis, perm)
        pair = jnp.stack([work, got])
        first = lax.dynamic_index_in_dim(pair, side, keepdims=False)
        second = lax.dynamic_index_in_dim(pair, 1 - side, keepdims=False)
        work = jnp.concatenate([first, second], axis=0)
    return work[:length].astype(jnp.float32)


def doubling_sum(values, axis):
    size = lax.axis_size(axis)
    for bit in range(size.bit_length() - 1):
        perm = [(i, i ^ (1 << bit)) for i in range(size)]
        got = lax.ppermute(values, axis, perm)
        values = tuple(a + b for a, b in zip(values, got))
    return values


def body(
    features,
    frame_count,
    norm1_gain,
    norm1_shift,
    qkv_weight,
    qkv_bias,
    out_weight,
    out_bias,
    norm2_gain,
    norm2_shift,
    conv_weight,
    conv_bias,
    cotangent,
):
    chans, clips, frames, rows, cols = features.shape
    groups = GROUPS // lax.axis_size("ch")
    mask = frame_mask(frame_count, frames)
    count = frame_count.astype(jnp.float32) * (chans // groups * rows * lax.axis_size("ha") * cols)
    first, second = moments(features, mask, groups)
    first, second = doubling_sum((first, second), "ha")
    normed = normalize(features, first, second, count, norm1_gain, norm1_shift, groups).astype(
        jnp.bfloat16
    )
    by_frame = lax.all_to_all(normed, "ch", split_axis=2, concat_axis=0, tiled=True)
    width = by_frame.shape[0]
    items = clips * by_frame.shape[2]
    tok_rows = rows * cols
    tokens = by_frame.reshape(width, items, tok_rows)
    queries = lax.dot_general(
        tokens, qkv_weight[:, :width], (((0,), (0,)), ((), ())), preferred_element_type=jnp.float32
    )
    queries = (queries + qkv_bias[:width]).astype(jnp.bfloat16)
    scale = width ** (-0.5)
    start_carry = (
        jnp.full((items, tok_rows), -jnp.inf, jnp.float32),
        jnp.zeros((items, tok_rows), jnp.float32),
        jnp.zeros((items, tok_rows, width), jnp.float32),
    )
    pairs = lax.dot_general(
        tokens, qkv_weight[:, width:], (((0,), (0,)), ((), ())), preferred_element_type=jnp.float32
    )
    pairs = (pairs + qkv_bias[width:]).astype(jnp.bfloat16)
    piece = lax.all_gather(pairs, "ha", axis=1, tiled=True)
    top, total, acc = attend(start_carry, queries, piece[..., :width], piece[..., width:], scale)
    attended = (acc / total[..., None]).astype(jnp.bfloat16)
    projected = lax.dot_general(
        out_weight, attended, (((0,), (2,)), ((), ())), preferred_element_type=jnp.float32
    )
    projected = (projected + out_bias[:, None, None]).astype(jnp.bfloat16).reshape(by_frame.shape)
    update = lax.all_to_all(projected, "ch", split_axis=0, concat_axis=2, tiled=True)
    hidden = (features.astype(jnp.float32) + update.astype(jnp.float32)).astype(jnp.bfloat16)
    first, second = moments(hidden, mask, groups)
    first, second = doubling_sum((first, second), "ha")
    gated = jax.nn.silu(
        normalize(hidden, first, second, count, norm2_gain, norm2_shift, groups)
    ).astype(jnp.bfloat16)
    with_rows = padded_2(gated, (("ha", 3),), 1)
    padded = jnp.pad(with_rows, ((0, 0), (0, 0), (2, 0), (0, 0), (1, 1)))
    stacks = [tap_stack(padded, time_tap, frames, rows, cols) for time_tap in range(3)]
    amount = chans * lax.axis_size("ch")
    summed = jnp.zeros((amount, clips, frames, rows, cols), jnp.float32)
    for time_tap in range(3):
        part = conv_weight[time_tap].reshape(9 * chans, amount)
        summed = summed + lax.dot_general(
            part, stacks[time_tap], (((0,), (0,)), ((), ())), preferred_element_type=jnp.float32
        )
    summed, stacks = lax.optimization_barrier((summed.astype(jnp.bfloat16), stacks))
    shares = lax.axis_size("ch")
    parts = summed.reshape((shares, amount // shares) + summed.shape[1:])
    parts = lax.all_to_all(parts, "ch", split_axis=0, concat_axis=0, tiled=True)
    conv_out = jnp.sum(parts.astype(jnp.float32), axis=0)
    mixed = mask[None, :, :, None, None] * (
        hidden.astype(jnp.float32) + conv_out + conv_bias[:, None, None, None, None]
    )
    mixed = mixed.astype(jnp.bfloat16)
    masked_cot = cotangent * mask.astype(jnp.bfloat16)[None, :, :, None, None]
    full_width = chans * lax.axis_size("ch")
    carry = jnp.zeros((3, 9 * chans, full_width), jnp.float32)
    copies = jnp.broadcast_to(masked_cot[None], (shares,) + masked_cot.shape)
    piece = lax.all_to_all(copies, "ch", split_axis=0, concat_axis=0, tiled=True)
    piece = piece.reshape((shares * chans,) + masked_cot.shape[1:])
    start = jnp.int32(0)
    for time_tap in range(3):
        part = lax.dot_general(
            stacks[time_tap],
            piece,
            (((1, 2, 3, 4), (1, 2, 3, 4)), ((), ())),
            preferred_element_type=jnp.float32,
        )
        carry = lax.dynamic_update_slice(
            carry, part[None], (jnp.int32(time_tap), jnp.int32(0), start)
        )
    weight_grad = butterfly_sum(carry.reshape(27 * chans, full_width), ("dp", "ha"))
    weight_grad = weight_grad.reshape(3, 3, 3, chans, full_width)
    return (mixed, weight_grad)


MESH = pl.DeviceIdType.MESH
HIGH = lax.Precision.HIGHEST
SEMS = 128
TAPS = 27
RUNS = ((0, 8), (8, 8), (16, 8), (24, 4))


def fits_fused(mesh):
    return mesh.shape["ch"] == 4 and mesh.shape["ha"] == 2 and mesh.shape["dp"] == 4


def nt_dot(a, b, precision=None):
    return lax.dot_general(
        a, b, (((1,), (1,)), ((), ())), preferred_element_type=jnp.float32, precision=precision
    )


def nn_dot(a, b, precision=None):
    return lax.dot_general(
        a, b, (((1,), (0,)), ((), ())), preferred_element_type=jnp.float32, precision=precision
    )


def column_of(row):
    parts = []
    for k in range(row.shape[1] // 128):
        block = jnp.broadcast_to(row[:, k * 128 : (k + 1) * 128], (128, 128))
        parts.append(block.T)
    return parts[0] if len(parts) == 1 else jnp.concatenate(parts, axis=0)


def wide(column):
    return jnp.concatenate([column, column], axis=1)


def group_sums(blocks, masks, groups):
    chans = blocks[0].shape[0]
    first = second = None
    for block, keep in zip(blocks, masks):
        one = block[:, :128] + block[:, 128:]
        sq = block * block
        two = sq[:, :128] + sq[:, 128:]
        first = one * keep if first is None else first + one * keep
        second = two * keep if second is None else second + two * keep
    ones = jnp.ones((8, 128), jnp.float32)
    size = chans // groups
    row = lax.broadcasted_iota(jnp.int32, (chans, 128), 0)
    lane = lax.broadcasted_iota(jnp.int32, (chans, 128), 1)
    row_group = jnp.zeros((chans, 128), jnp.int32)
    lane_group = jnp.zeros((chans, 128), jnp.int32)
    for g in range(1, groups):
        row_group = row_group + (row >= g * size).astype(jnp.int32)
        lane_group = lane_group + (lane >= g * size).astype(jnp.int32)
    same = ((row_group == lane_group) & (lane < chans)).astype(jnp.float32)
    sums = nt_dot(ones, first, HIGH)
    squares = nt_dot(ones, second, HIGH)
    return nn_dot(sums, same, HIGH), nn_dot(squares, same, HIGH)


def fused_kernel(
    groups,
    all_rows,
    fc_ref,
    feat_any,
    cot_any,
    n1g_any,
    n1s_any,
    n2g_any,
    n2s_any,
    cb_any,
    qkvb_any,
    ob_any,
    wq_any,
    wo_any,
    wc_any,
    mixed_ref,
    grad_ref,
    feat_in,
    cot_in,
    n1g_in,
    n1s_in,
    n2g_in,
    n2s_in,
    cb_in,
    qkvb_in,
    ob_in,
    rows_ref,
    feat_ref,
    wq_ref,
    wo_ref,
    wc_ref,
    wqt_ref,
    wot_ref,
    wct_ref,
    qkvb_col,
    ob_col,
    cb_col,
    stat_ref,
    raw_ref,
    nrm_ref,
    qkv_ref,
    upd_s,
    upd_r,
    stat2_ref,
    halo_s,
    halo_r,
    hid_ref,
    stack_ref,
    cot_all,
    conv_s,
    conv_r,
    gate_s,
    gate_r,
    taps_ref,
    acc_ref,
    sum_s,
    sum_r,
    res_ref,
    send_sem,
    recv_sem,
    local_sem,
):
    frames, chans, span = feat_ref.shape
    nch = 4
    full = nch * chans
    z = lax.axis_index("ch")
    x = lax.axis_index("ha")
    d = lax.axis_index("dp")
    core = lax.rem(d, 2)
    yy = lax.div(d, 2)
    core_peer = {"dp": d + 1 - 2 * core}
    y_peer = {"dp": lax.rem(d + 2, 4)}
    x_peer = {"ha": 1 - x}
    count_f = fc_ref[0]
    masks = [jnp.where(f < count_f, 1.0, 0.0).astype(jnp.float32) for f in range(frames)]

    counter = [0]
    pending = []

    def copy_to(src, dst, dev, start=True):
        k = counter[0]
        counter[0] += 1
        c = pltpu.make_async_remote_copy(
            src_ref=src,
            dst_ref=dst,
            send_sem=send_sem.at[k],
            recv_sem=recv_sem.at[k],
            device_id=dev,
            device_id_type=MESH,
        )
        if start:
            c.start()
            pending.append(c)
        return c, k

    def arrived(dst, k):
        pltpu.make_async_remote_copy(
            src_ref=dst,
            dst_ref=dst,
            send_sem=send_sem.at[k],
            recv_sem=recv_sem.at[k],
            device_id=x_peer,
            device_id_type=MESH,
        ).wait_recv()

    loads = {}
    for k, (name, a, b) in enumerate(
        (
            ("feat", feat_any, feat_in),
            ("n1g", n1g_any, n1g_in),
            ("n1s", n1s_any, n1s_in),
            ("qkvb", qkvb_any, qkvb_in),
            ("ob", ob_any, ob_in),
            ("wq", wq_any, wq_ref),
            ("cot", cot_any, cot_in),
            ("wo", wo_any, wo_ref),
            ("wc", wc_any, wc_ref),
            ("n2g", n2g_any, n2g_in),
            ("n2s", n2s_any, n2s_in),
            ("cb", cb_any, cb_in),
        )
    ):
        loads[name] = pltpu.make_async_copy(a, b, local_sem.at[k])
        loads[name].start()

    barrier = pltpu.get_barrier_semaphore()
    ahead = [lax.rem(z + j, nch) for j in range(nch)]
    behind = [lax.rem(z + nch - j, nch) for j in range(nch)]
    diag_peer = {"dp": 3 - d}
    partners = [core_peer, y_peer, x_peer, diag_peer]
    for j in range(1, nch):
        partners.append({"ch": ahead[j]})
        partners.append({"ch": ahead[j], "ha": 1 - x})
    for dev in partners:
        pl.semaphore_signal(barrier, inc=1, device_id=dev, device_id_type=MESH)

    def row_block(f, r):
        return rows_ref[pl.ds(f * 2 + r, chans, stride=2 * frames), :]

    loads["feat"].wait()
    rows_ref[...] = feat_in[...].astype(jnp.float32)
    for f in range(frames):
        for r in range(2):
            feat_ref[f, :, r * 128 : (r + 1) * 128] = row_block(f, r).astype(jnp.bfloat16)

    first, second = group_sums(
        [feat_ref[f].astype(jnp.float32) for f in range(frames)], masks, groups
    )
    loads["n1g"].wait()
    loads["n1s"].wait()
    lanes_pad = jnp.zeros((1, 128 - chans), jnp.float32)
    own = stat_ref.at[0, z]
    own[...] = jnp.zeros((8, 128), jnp.float32)
    own[0:1, :] = first[0:1, :]
    own[1:2, :] = second[0:1, :]
    own[2:3, :] = jnp.concatenate([n1g_in[...].reshape(1, chans), lanes_pad], axis=1)
    own[3:4, :] = jnp.concatenate([n1s_in[...].reshape(1, chans), lanes_pad], axis=1)

    pl.semaphore_wait(barrier, len(partners))

    feat_k = {}
    for j in range(1, nch):
        _, feat_k[j] = copy_to(feat_ref.at[ahead[j]], raw_ref.at[0, z], {"ch": ahead[j]})
    _, feat_own_k = copy_to(feat_ref.at[z], raw_ref.at[1, z], x_peer)
    stat_k = []
    for j in range(nch):
        if j:
            _, k = copy_to(stat_ref.at[0, z], stat_ref.at[0, z], {"ch": ahead[j]})
            stat_k.append((0, j, k))
        _, k = copy_to(stat_ref.at[0, z], stat_ref.at[1, z], {"ch": ahead[j], "ha": 1 - x})
        stat_k.append((1, j, k))
    raw_ref[0, z] = feat_ref[z]

    line_k = {}
    shards = []

    def shard(slot, c):
        return cot_all.at[slot, pl.ds(pl.multiple_of(c * chans, chans), chans)]

    def line_step(step):
        low, high = z - step + 1, z + step - 1
        to_up, to_down = {"ch": lax.rem(z + 1, nch)}, {"ch": lax.rem(z + nch - 1, nch)}
        up, ku = copy_to(shard(0, low), shard(0, low), to_up, start=False)
        down, kd = copy_to(shard(0, high), shard(0, high), to_down, start=False)
        line_k[step] = (up, ku, down, kd)

        @pl.when((low >= 0) & (z + 1 < nch))
        def _():
            up.start()

        @pl.when((high < nch) & (z >= 1))
        def _():
            down.start()

    def spread(c, k, valid):
        on_y, ky = copy_to(shard(0, c), shard(2, c), y_peer, start=False)
        on_core, kc = copy_to(shard(0, c), shard(1, c), core_peer, start=False)
        on_far, kf = copy_to(shard(2, c), shard(3, c), core_peer, start=False)
        shards.append((c, valid, on_y, ky, on_core, kc, on_far, kf))

        @pl.when(valid)
        def _():
            if k is not None:
                arrived(shard(0, c), k)
            on_y.start()
            on_core.start()

    def line_wait(step):
        _, ku, _, kd = line_k[step]
        spread(z - step, ku, z - step >= 0)
        spread(z + step, kd, z + step < nch)

    def pass_on(n):
        c, valid, _, ky, _, _, on_far, _ = shards[n]

        @pl.when(valid)
        def _():
            arrived(shard(2, c), ky)
            on_far.start()

    def gathered():
        for c, valid, _, _, _, kc, _, kf in shards:

            @pl.when(valid)
            def _(c=c, kc=kc, kf=kf):
                arrived(shard(1, c), kc)
                arrived(shard(3, c), kf)

    def line_finish(step):
        up, _, down, _ = line_k[step]

        @pl.when((z - step + 1 >= 0) & (z + 1 < nch))
        def _():
            up.wait_send()

        @pl.when((z + step - 1 < nch) & (z >= 1))
        def _():
            down.wait_send()

    def shards_finish():
        for _, valid, on_y, _, on_core, _, on_far, _ in shards:

            @pl.when(valid)
            def _(on_y=on_y, on_core=on_core, on_far=on_far):
                on_y.wait_send()
                on_core.wait_send()
                on_far.wait_send()

    loads["cot"].wait()
    own_rows = pl.ds(pl.multiple_of(z * chans, chans), chans)
    rows_ref[...] = cot_in[...].astype(jnp.float32)
    for f in range(frames):
        for r in range(2):
            at = f * span + r * 128
            cot_all[0, own_rows, at : at + 128] = (row_block(f, r) * masks[f]).astype(jnp.bfloat16)
    spread(z, None, z >= 0)
    line_step(1)
    for name in ("qkvb", "ob", "cb", "n2g", "n2s"):
        loads[name].wait()
    qkvb_col[...] = column_of(qkvb_in[...].reshape(1, 3 * full))
    ob_col[...] = column_of(ob_in[...].reshape(1, full))
    cb_row = cb_in[...].reshape(1, chans)
    cb_col[...] = column_of(jnp.concatenate([cb_row, lanes_pad], axis=1))[:chans]
    stack_ref[:, 0 : 2 * span] = jnp.zeros((9 * chans, 2 * span), jnp.bfloat16)
    size = chans // 4
    for slot in range(4):
        taps_ref[slot, :, 0 : 2 * span] = jnp.zeros((9 * size, 2 * span), jnp.bfloat16)
    fwd_k = {}
    for j in range(1, nch):
        zs = behind[j]
        arrived(raw_ref.at[0, zs], feat_k[j])
        _, fwd_k[j] = copy_to(raw_ref.at[0, zs], raw_ref.at[1, zs], x_peer)

    loads["wq"].wait()
    loads["wo"].wait()
    for k in range(9):
        wqt_ref[k * 128 : (k + 1) * 128, :] = wq_ref[:, k * 128 : (k + 1) * 128].T
    for k in range(3):
        wot_ref[k * 128 : (k + 1) * 128, :] = wo_ref[:, k * 128 : (k + 1) * 128].T


    for side, j, k in stat_k:
        arrived(stat_ref.at[side, behind[j]], k)
    entries = count_f.astype(jnp.float32) * float(chans // groups * all_rows * 128)

    def norm_columns(total, total_sq, gain, shift):
        mean = total / entries
        var = total_sq / entries - mean * mean
        scale = lax.rsqrt(var + EPS) * gain
        return [wide(column_of(v)[:chans]) for v in (mean, scale, shift)]

    cols = []
    for c in range(nch):
        both = stat_ref[0, c] + stat_ref[1, c]
        cols.append(
            norm_columns(both[0:1], both[1:2], stat_ref[0, c, 2:3], stat_ref[0, c, 3:4])
        )

    def normalize_side(side):
        for c in range(nch):
            mean, scale, shift = cols[c]
            block = raw_ref[side, c].astype(jnp.float32)
            nrm_ref[c * chans : (c + 1) * chans, side * span : (side + 1) * span] = (
                (block - mean) * scale + shift
            ).astype(jnp.bfloat16)

    normalize_side(0)
    bias = wide(qkvb_col[...])
    qkv_ref[:, 0:span] = (nn_dot(wqt_ref[...], nrm_ref[:, 0:span]) + bias).astype(jnp.bfloat16)
    arrived(raw_ref.at[1, z], feat_own_k)
    for j in range(1, nch):
        arrived(raw_ref.at[1, behind[j]], fwd_k[j])
    normalize_side(1)
    qkv_ref[full:, span:] = (
        nn_dot(wqt_ref[full:, :], nrm_ref[:, span:]) + bias[full:]
    ).astype(jnp.bfloat16)

    keys = qkv_ref[full : 2 * full, :].T
    scores = nn_dot(keys, qkv_ref[0:full, 0:span]) * (full ** (-0.5))
    line_wait(1)
    line_step(2)
    top = jnp.max(scores, axis=0, keepdims=True)
    weights = jnp.exp(scores - top)
    total = jnp.sum(weights, axis=0, keepdims=True)
    attended = nn_dot(qkv_ref[2 * full :, :], weights.astype(jnp.bfloat16)) / total
    update = nn_dot(wot_ref[...], attended.astype(jnp.bfloat16)) + wide(ob_col[...])
    update = update.astype(jnp.bfloat16)
    for c in range(nch):
        upd_s[c] = update[c * chans : (c + 1) * chans]
    upd_k = {}
    for j in range(1, nch):
        _, upd_k[j] = copy_to(upd_s.at[ahead[j]], upd_r.at[z], {"ch": ahead[j]})
    upd_r[z] = upd_s[z]

    loads["wc"].wait()
    for k in range(0, TAPS * chans, 128):
        stop = min(k + 128, TAPS * chans)
        wct_ref[:, k:stop] = wc_ref[k:stop, :].T

    for j in range(1, nch):
        arrived(upd_r.at[behind[j]], upd_k[j])
    line_wait(2)
    line_step(3)
    pass_on(0)

    hidden = []
    for f in range(frames):
        h = (feat_ref[f].astype(jnp.float32) + upd_r[f].astype(jnp.float32)).astype(jnp.bfloat16)
        hid_ref[f] = h
        hidden.append(h.astype(jnp.float32))
        halo_s[f] = jnp.where(x == 0, h[:, 128:], h[:, :128])
    _, halo_k = copy_to(halo_s, halo_r, x_peer)
    first, second = group_sums(hidden, masks, groups)
    stat2_ref[0] = jnp.zeros((8, 128), jnp.float32)
    stat2_ref[0, 0:1, :] = first[0:1, :]
    stat2_ref[0, 1:2, :] = second[0:1, :]
    _, stat2_k = copy_to(stat2_ref.at[0], stat2_ref.at[1], x_peer)
    arrived(stat2_ref.at[1], stat2_k)
    both = stat2_ref[0] + stat2_ref[1]
    gain2 = jnp.concatenate([n2g_in[...].reshape(1, chans), lanes_pad], axis=1)
    shift2 = jnp.concatenate([n2s_in[...].reshape(1, chans), lanes_pad], axis=1)
    mean2, scale2, shift2 = norm_columns(both[0:1], both[1:2], gain2, shift2)
    mean2, scale2, shift2 = mean2[:, :128], scale2[:, :128], shift2[:, :128]
    lane = lax.broadcasted_iota(jnp.int32, (chans, 128), 1)

    def place(f, row, values):
        left = jnp.where(lane == 0, 0.0, pltpu.roll(values, 1, 1)).astype(jnp.bfloat16)
        right = jnp.where(lane == 127, 0.0, pltpu.roll(values, 127, 1)).astype(jnp.bfloat16)
        centre = values.astype(jnp.bfloat16)
        for row_tap in range(3):
            out_row = row + 1 - row_tap
            if out_row < 0 or out_row > 1:
                continue
            at = (f + 2) * span + out_row * 128
            for col_tap, v in enumerate((left, centre, right)):
                tap = row_tap * 3 + col_tap
                stack_ref[tap * chans : (tap + 1) * chans, at : at + 128] = v

    part = chans // 4
    half_frames = frames // 2

    def slice_at(f, block):
        at = (f % half_frames * 3 + block) * 128
        return f // half_frames * part, at

    def keep_slices(f, block, values):
        row, at = slice_at(f, block)
        for g in range(4):
            gate_s[g, row : row + part, at : at + 128] = values[g * part : (g + 1) * part].astype(
                jnp.bfloat16
            )

    def gate(values):
        u = (values - mean2) * scale2 + shift2
        return u / (1.0 + jnp.exp(-u))

    for f in range(frames):
        for r in range(2):
            values = gate(hid_ref[f, :, r * 128 : (r + 1) * 128].astype(jnp.float32))
            keep_slices(f, r, values)
            place(f, r, values)
    line_wait(3)
    for n in range(1, 3):
        pass_on(n)
    arrived(halo_r, halo_k)
    for f in range(frames):
        values = gate(halo_r[f].astype(jnp.float32))
        keep_slices(f, 2, values)
        place(f, -1, jnp.where(x == 1, values, 0.0))
        place(f, 2, jnp.where(x == 0, values, 0.0))
    gate_k = []
    for slot, dev, g in ((1, core_peer, d + 1 - 2 * core), (2, y_peer, lax.rem(d + 2, 4)), (3, diag_peer, 3 - d)):
        _, k = copy_to(gate_s.at[g], gate_r.at[slot], dev)
        gate_k.append((slot, k))
    gate_r[0] = gate_s[d]


    conv_k = {}

    def conv_frame(f):
        acc = None
        for kt in range(3):
            term = nn_dot(
                wct_ref[:, kt * 9 * chans : (kt + 1) * 9 * chans],
                stack_ref[:, (f + kt) * span : (f + kt + 1) * span],
            )
            acc = term if acc is None else acc + term
        acc = acc.astype(jnp.bfloat16)
        for c in range(nch):
            conv_s[f, c] = acc[c * chans : (c + 1) * chans]
        for j in range(1, nch):
            _, conv_k[f, j] = copy_to(
                conv_s.at[f, ahead[j]], conv_r.at[f, z], {"ch": ahead[j]}
            )

    for f in range(frames):
        conv_frame(f)
    for slot, k in gate_k:
        arrived(gate_r.at[slot], k)
    lane = lax.broadcasted_iota(jnp.int32, (part, 128), 1)
    for slot in range(4):
        for f in range(frames):
            for block in range(3):
                row, at = slice_at(f, block)
                values = gate_r[slot, row : row + part, at : at + 128].astype(jnp.float32)
                windows = (
                    jnp.where(lane == 0, 0.0, pltpu.roll(values, 1, 1)),
                    values,
                    jnp.where(lane == 127, 0.0, pltpu.roll(values, 127, 1)),
                )
                if block < 2:
                    spots = [(block, windows)]
                else:
                    spots = [
                        (-1, [jnp.where(x == 1, v, 0.0) for v in windows]),
                        (2, [jnp.where(x == 0, v, 0.0) for v in windows]),
                    ]
                for row, three in spots:
                    three = [v.astype(jnp.bfloat16) for v in three]
                    for row_tap in range(3):
                        out_row = row + 1 - row_tap
                        if out_row < 0 or out_row > 1:
                            continue
                        at = (f + 2) * span + out_row * 128
                        for col_tap in range(3):
                            tap = row_tap * 3 + col_tap
                            taps_ref[slot, tap * part : (tap + 1) * part, at : at + 128] = three[
                                col_tap
                            ]

    acc_ref[TAPS * part :, :] = jnp.zeros((part, full), jnp.float32)
    for n in range(3, 7):
        pass_on(n)
    gathered()

    def grad_taps(kt):
        value = None
        for slot in range(4):
            term = nt_dot(
                taps_ref[slot, :, kt * span : (kt + frames) * span], cot_all[slot]
            )
            value = term if value is None else value + term
        acc_ref[9 * part * kt : 9 * part * (kt + 1), :] = value

    def rows_at(c, side):
        first, taps = RUNS[c]
        count = taps // 2 * part
        return pl.ds(pl.multiple_of(first * part + side * count, count), count)

    def run_rows(c):
        first, taps = RUNS[c]
        return slice(first * part, (first + taps) * part)

    run_k = [dict() for _ in RUNS]

    def sum_send(c):
        count = RUNS[c][1] // 2 * part
        sum_s[c, 0:count] = acc_ref[rows_at(c, 1 - x), :].astype(jnp.bfloat16)
        _, run_k[c]["sum"] = copy_to(sum_s.at[c, 0:count], sum_r.at[c, 0:count], x_peer)

    def piece(c, g, side):
        return res_ref.at[g, rows_at(c, side)]

    g_core, g_y, g_far = d + 1 - 2 * core, lax.rem(d + 2, 4), 3 - d

    def deliver(c, g):
        first, taps = RUNS[c]
        for t in range(first, min(first + taps, TAPS)):
            grad_ref[t, pl.ds(pl.multiple_of(g * part, 8), part), :] = res_ref[
                g, t * part : (t + 1) * part, :
            ].astype(jnp.float32)

    def sum_done(c):
        count = RUNS[c][1] // 2 * part
        arrived(sum_r.at[c, 0:count], run_k[c]["sum"])
        total = acc_ref[rows_at(c, x), :] + sum_r[c, 0:count].astype(jnp.float32)
        res_ref[d, rows_at(c, x), :] = total.astype(jnp.bfloat16)
        own = piece(c, d, x)
        _, run_k[c]["x"] = copy_to(own, own, x_peer)
        _, run_k[c]["y0"] = copy_to(own, own, y_peer)
        _, run_k[c]["core0"] = copy_to(own, own, core_peer)

    def pass_x(c):
        other = piece(c, d, 1 - x)
        arrived(other, run_k[c]["x"])
        _, run_k[c]["y1"] = copy_to(other, other, y_peer)
        _, run_k[c]["core1"] = copy_to(other, other, core_peer)
        deliver(c, d)

    def pass_y(c):
        arrived(piece(c, g_y, x), run_k[c]["y0"])
        arrived(piece(c, g_y, 1 - x), run_k[c]["y1"])
        whole = res_ref.at[g_y, run_rows(c)]
        _, run_k[c]["far"] = copy_to(whole, whole, core_peer)
        deliver(c, g_y)

    def finish(c):
        arrived(piece(c, g_core, x), run_k[c]["core0"])
        arrived(piece(c, g_core, 1 - x), run_k[c]["core1"])
        deliver(c, g_core)
        arrived(res_ref.at[g_far, run_rows(c)], run_k[c]["far"])
        deliver(c, g_far)

    grad_taps(0)
    sum_send(0)
    grad_taps(1)
    sum_send(1)
    sum_done(0)
    grad_taps(2)
    sum_send(2)
    sum_send(3)
    sum_done(1)
    pass_x(0)
    sum_done(2)
    pass_x(1)
    sum_done(3)
    pass_y(0)
    pass_x(2)
    pass_y(1)
    pass_x(3)
    conv_bias = wide(cb_col[...])
    for f in range(frames):
        total = hid_ref[f].astype(jnp.float32) + conv_bias
        for j in range(1, nch):
            arrived(conv_r.at[f, behind[j]], conv_k[f, j])
        total = total + conv_s[f, z].astype(jnp.float32)
        for j in range(1, nch):
            total = total + conv_r[f, behind[j]].astype(jnp.float32)
        total = total * masks[f]
        for r in range(2):
            rows_ref[pl.ds(f * 2 + r, chans, stride=2 * frames), :] = total[
                :, r * 128 : (r + 1) * 128
            ]
    mixed_ref[...] = rows_ref[...].astype(jnp.bfloat16)
    finish(0)
    pass_y(2)
    finish(1)
    pass_y(3)
    finish(2)
    finish(3)

    for c in pending:
        c.wait_send()
    shards_finish()
    for step in line_k:
        line_finish(step)


def fused_body(
    features,
    frame_count,
    norm1_gain,
    norm1_shift,
    qkv_weight,
    qkv_bias,
    out_weight,
    out_bias,
    norm2_gain,
    norm2_shift,
    conv_weight,
    conv_bias,
    cotangent,
):
    chans, clips, frames, rows, cols = features.shape
    nch = lax.axis_size("ch")
    full = nch * chans
    span = rows * cols
    groups = GROUPS // nch

    bf16, f32 = jnp.bfloat16, jnp.float32
    vm = pltpu.VMEM
    vmem = pl.BlockSpec(memory_space=pltpu.VMEM)
    hbm = pl.BlockSpec(memory_space=pltpu.HBM)
    lines = (chans * frames * rows, cols)
    scratch = [
        vm(lines, bf16),
        vm(lines, bf16),
        vm((chans,), f32),
        vm((chans,), f32),
        vm((chans,), f32),
        vm((chans,), f32),
        vm((chans,), f32),
        vm((3 * full,), f32),
        vm((full,), f32),
        vm(lines, f32),
        vm((frames, chans, span), bf16),
        vm((full, 3 * full), bf16),
        vm((full, full), bf16),
        vm((TAPS * chans, full), bf16),
        vm((3 * full, full), bf16),
        vm((full, full), bf16),
        vm((full, TAPS * chans), bf16),
        vm((3 * full, 128), f32),
        vm((full, 128), f32),
        vm((chans, 128), f32),
        vm((2, nch, 8, 128), f32),
        vm((2, nch, chans, span), bf16),
        vm((full, 2 * span), bf16),
        vm((3 * full, 2 * span), bf16),
        vm((nch, chans, span), bf16),
        vm((nch, chans, span), bf16),
        vm((2, 8, 128), f32),
        vm((frames, chans, 128), bf16),
        vm((frames, chans, 128), bf16),
        vm((frames, chans, span), bf16),
        vm((9 * chans, (frames + 2) * span), bf16),
        vm((4, full, frames * span), bf16),
        vm((frames, nch, chans, span), bf16),
        vm((frames, nch, chans, span), bf16),
        vm((4, chans // 2, frames // 2 * 3 * cols), bf16),
        vm((4, chans // 2, frames // 2 * 3 * cols), bf16),
        vm((4, 9 * (chans // 4), (frames + 2) * span), bf16),
        vm(((TAPS + 1) * (chans // 4), full), f32),
        vm((len(RUNS), chans, full), bf16),
        vm((len(RUNS), chans, full), bf16),
        vm((4, (TAPS + 1) * (chans // 4), full), bf16),
        pltpu.SemaphoreType.DMA((SEMS,)),
        pltpu.SemaphoreType.DMA((SEMS,)),
        pltpu.SemaphoreType.DMA((12,)),
    ]
    operands = (
        features.reshape(lines),
        cotangent.reshape(lines),
        norm1_gain,
        norm1_shift,
        norm2_gain,
        norm2_shift,
        conv_bias,
        qkv_bias,
        out_bias,
        qkv_weight,
        out_weight,
        conv_weight.reshape(TAPS * chans, full),
    )
    mixed, grad = pl.pallas_call(
        functools.partial(fused_kernel, groups, rows * lax.axis_size("ha")),
        out_shape=(
            jax.ShapeDtypeStruct(lines, bf16),
            jax.ShapeDtypeStruct((TAPS, chans, full), f32),
        ),
        in_specs=[pl.BlockSpec(memory_space=pltpu.SMEM)] + [hbm] * 12,
        out_specs=(vmem, vmem),
        scratch_shapes=scratch,
        compiler_params=pltpu.CompilerParams(
            collective_id=0, has_side_effects=True, vmem_limit_bytes=40 * 1024 * 1024
        ),
    )(
        frame_count,
        *(pltpu.with_memory_space_constraint(v, pltpu.HBM) for v in operands),
    )
    mixed = mixed.reshape(chans, clips, frames, rows, cols)
    grad = grad.reshape(3, 3, 3, chans, full)
    return mixed, grad


def solution(mesh):
    placed = (
        P("ch", "dp", None, "ha", None),
        P("dp"),
        P("ch"),
        P("ch"),
        P(),
        P(),
        P(),
        P(),
        P("ch"),
        P("ch"),
        P(None, None, None, "ch", None),
        P("ch"),
        P("ch", "dp", None, "ha", None),
    )
    return jax.shard_map(
        fused_body if fits_fused(mesh) else body,
        mesh=mesh,
        in_specs=placed,
        out_specs=(P("ch", "dp", None, "ha", None), P(None, None, None, "ch", None)),
        check_vma=False,
    )
```

```python
import functools

import jax
import jax.numpy as jnp
from jax import lax
from jax.experimental import pallas as pl
from jax.experimental.pallas import tpu as pltpu
from jax.sharding import PartitionSpec as P

GROUPS = 32


EPS = 1e-06


def padded_2(x, sides, width):
    for axis, dim in sides:
        count, length = (lax.axis_size(axis), x.shape[dim])
        up = [(i, (i + 1) % count) for i in range(count - 1)]
        down = [(j, i) for i, j in up]
        last = lax.slice_in_dim(x, length - width, length, axis=dim)
        leading = lax.slice_in_dim(x, 0, width, axis=dim)
        before = lax.ppermute(last, axis, up)
        after = lax.ppermute(leading, axis, down)
        x = jnp.concatenate([before, x, after], axis=dim)
    return x


def frame_mask(frame_count, frames):
    position = lax.broadcasted_iota(jnp.int32, (frame_count.shape[0], frames), 1)
    return (position < frame_count[:, None]).astype(jnp.float32)


def moments(values, mask, groups):
    chans, clips, frames, rows, cols = values.shape
    data = values.astype(jnp.float32).reshape(groups, chans // groups, clips, frames, rows * cols)
    first = jnp.einsum("gkbfp,bf->gb", data, mask)
    second = jnp.einsum("gkbfp,bf->gb", data * data, mask)
    return (first, second)


def normalize(values, first, second, count, gain, shift, groups):
    chans, clips, frames, rows, cols = values.shape
    mean = first / count[None, :]
    var = second / count[None, :] - mean * mean
    scale = lax.rsqrt(var + EPS)
    data = values.astype(jnp.float32).reshape(groups, chans // groups, clips, frames, rows * cols)
    normed = (data - mean[:, None, :, None, None]) * scale[:, None, :, None, None]
    normed = normed.reshape(values.shape)
    return normed * gain[:, None, None, None, None] + shift[:, None, None, None, None]


def attend(carry, queries, keys, values, scale):
    top, total, acc = carry
    scores = jnp.einsum("itc,isc->its", queries, keys, preferred_element_type=jnp.float32) * scale
    new_top = jnp.max(scores, axis=2)
    factor = jnp.exp(top - new_top)
    weights = jnp.exp(scores - new_top[..., None])
    total = total * factor + jnp.sum(weights, axis=2)
    acc = acc * factor[..., None] + jnp.einsum(
        "its,isc->itc", weights.astype(jnp.bfloat16), values, preferred_element_type=jnp.float32
    )
    return (new_top, total, acc)


def tap_stack(padded, time_tap, frames, rows, cols):
    windows = []
    for row_tap in range(3):
        for col_tap in range(3):
            windows.append(
                padded[
                    :,
                    :,
                    time_tap : time_tap + frames,
                    row_tap : row_tap + rows,
                    col_tap : col_tap + cols,
                ]
            )
    return jnp.concatenate(windows, axis=0)


def butterfly_sum(table, axes):
    steps = []
    for axis in axes:
        size = lax.axis_size(axis)
        for bit in range(size.bit_length() - 1):
            steps.append((axis, bit, size))
    length = table.shape[0]
    unit = (1 << len(steps)) * 8
    padded = -(-length // unit) * unit
    work = jnp.pad(table, ((0, padded - length), (0, 0)))
    for axis, bit, size in steps:
        side = (lax.axis_index(axis) >> bit) & 1
        halves = work.reshape(2, work.shape[0] // 2, work.shape[1])
        keep = lax.dynamic_index_in_dim(halves, side, keepdims=False)
        send = lax.dynamic_index_in_dim(halves, 1 - side, keepdims=False)
        perm = [(i, i ^ (1 << bit)) for i in range(size)]
        got = lax.ppermute(send.astype(jnp.bfloat16), axis, perm)
        work = keep + got.astype(jnp.float32)
    work = work.astype(jnp.bfloat16)
    for axis, bit, size in reversed(steps):
        side = (lax.axis_index(axis) >> bit) & 1
        perm = [(i, i ^ (1 << bit)) for i in range(size)]
        got = lax.ppermute(work, axis, perm)
        pair = jnp.stack([work, got])
        first = lax.dynamic_index_in_dim(pair, side, keepdims=False)
        second = lax.dynamic_index_in_dim(pair, 1 - side, keepdims=False)
        work = jnp.concatenate([first, second], axis=0)
    return work[:length].astype(jnp.float32)


def doubling_sum(values, axis):
    size = lax.axis_size(axis)
    for bit in range(size.bit_length() - 1):
        perm = [(i, i ^ (1 << bit)) for i in range(size)]
        got = lax.ppermute(values, axis, perm)
        values = tuple(a + b for a, b in zip(values, got))
    return values


def body(
    features,
    frame_count,
    norm1_gain,
    norm1_shift,
    qkv_weight,
    qkv_bias,
    out_weight,
    out_bias,
    norm2_gain,
    norm2_shift,
    conv_weight,
    conv_bias,
    cotangent,
):
    chans, clips, frames, rows, cols = features.shape
    groups = GROUPS // lax.axis_size("ch")
    mask = frame_mask(frame_count, frames)
    count = frame_count.astype(jnp.float32) * (chans // groups * rows * lax.axis_size("ha") * cols)
    first, second = moments(features, mask, groups)
    first, second = doubling_sum((first, second), "ha")
    normed = normalize(features, first, second, count, norm1_gain, norm1_shift, groups).astype(
        jnp.bfloat16
    )
    by_frame = lax.all_to_all(normed, "ch", split_axis=2, concat_axis=0, tiled=True)
    width = by_frame.shape[0]
    items = clips * by_frame.shape[2]
    tok_rows = rows * cols
    tokens = by_frame.reshape(width, items, tok_rows)
    queries = lax.dot_general(
        tokens, qkv_weight[:, :width], (((0,), (0,)), ((), ())), preferred_element_type=jnp.float32
    )
    queries = (queries + qkv_bias[:width]).astype(jnp.bfloat16)
    scale = width ** (-0.5)
    start_carry = (
        jnp.full((items, tok_rows), -jnp.inf, jnp.float32),
        jnp.zeros((items, tok_rows), jnp.float32),
        jnp.zeros((items, tok_rows, width), jnp.float32),
    )
    pairs = lax.dot_general(
        tokens, qkv_weight[:, width:], (((0,), (0,)), ((), ())), preferred_element_type=jnp.float32
    )
    pairs = (pairs + qkv_bias[width:]).astype(jnp.bfloat16)
    piece = lax.all_gather(pairs, "ha", axis=1, tiled=True)
    top, total, acc = attend(start_carry, queries, piece[..., :width], piece[..., width:], scale)
    attended = (acc / total[..., None]).astype(jnp.bfloat16)
    projected = lax.dot_general(
        out_weight, attended, (((0,), (2,)), ((), ())), preferred_element_type=jnp.float32
    )
    projected = (projected + out_bias[:, None, None]).astype(jnp.bfloat16).reshape(by_frame.shape)
    update = lax.all_to_all(projected, "ch", split_axis=0, concat_axis=2, tiled=True)
    hidden = (features.astype(jnp.float32) + update.astype(jnp.float32)).astype(jnp.bfloat16)
    first, second = moments(hidden, mask, groups)
    first, second = doubling_sum((first, second), "ha")
    gated = jax.nn.silu(
        normalize(hidden, first, second, count, norm2_gain, norm2_shift, groups)
    ).astype(jnp.bfloat16)
    with_rows = padded_2(gated, (("ha", 3),), 1)
    padded = jnp.pad(with_rows, ((0, 0), (0, 0), (2, 0), (0, 0), (1, 1)))
    stacks = [tap_stack(padded, time_tap, frames, rows, cols) for time_tap in range(3)]
    amount = chans * lax.axis_size("ch")
    summed = jnp.zeros((amount, clips, frames, rows, cols), jnp.float32)
    for time_tap in range(3):
        part = conv_weight[time_tap].reshape(9 * chans, amount)
        summed = summed + lax.dot_general(
            part, stacks[time_tap], (((0,), (0,)), ((), ())), preferred_element_type=jnp.float32
        )
    summed, stacks = lax.optimization_barrier((summed.astype(jnp.bfloat16), stacks))
    shares = lax.axis_size("ch")
    parts = summed.reshape((shares, amount // shares) + summed.shape[1:])
    parts = lax.all_to_all(parts, "ch", split_axis=0, concat_axis=0, tiled=True)
    conv_out = jnp.sum(parts.astype(jnp.float32), axis=0)
    mixed = mask[None, :, :, None, None] * (
        hidden.astype(jnp.float32) + conv_out + conv_bias[:, None, None, None, None]
    )
    mixed = mixed.astype(jnp.bfloat16)
    masked_cot = cotangent * mask.astype(jnp.bfloat16)[None, :, :, None, None]
    full_width = chans * lax.axis_size("ch")
    carry = jnp.zeros((3, 9 * chans, full_width), jnp.float32)
    copies = jnp.broadcast_to(masked_cot[None], (shares,) + masked_cot.shape)
    piece = lax.all_to_all(copies, "ch", split_axis=0, concat_axis=0, tiled=True)
    piece = piece.reshape((shares * chans,) + masked_cot.shape[1:])
    start = jnp.int32(0)
    for time_tap in range(3):
        part = lax.dot_general(
            stacks[time_tap],
            piece,
            (((1, 2, 3, 4), (1, 2, 3, 4)), ((), ())),
            preferred_element_type=jnp.float32,
        )
        carry = lax.dynamic_update_slice(
            carry, part[None], (jnp.int32(time_tap), jnp.int32(0), start)
        )
    weight_grad = butterfly_sum(carry.reshape(27 * chans, full_width), ("dp", "ha"))
    weight_grad = weight_grad.reshape(3, 3, 3, chans, full_width)
    return (mixed, weight_grad)


MESH = pl.DeviceIdType.MESH
HIGH = lax.Precision.HIGHEST
SEMS = 128
TAPS = 27
CONV_FIRST = 2
STRAIGHT = 1
Y_FIRST = (2, 3)
RUNS = ((0, 8), (8, 8), (16, 8), (24, 4))


def fits_fused(mesh):
    return mesh.shape["ch"] == 4 and mesh.shape["ha"] == 2 and mesh.shape["dp"] == 4


def nt_dot(a, b, precision=None):
    return lax.dot_general(
        a, b, (((1,), (1,)), ((), ())), preferred_element_type=jnp.float32, precision=precision
    )


def nn_dot(a, b, precision=None):
    return lax.dot_general(
        a, b, (((1,), (0,)), ((), ())), preferred_element_type=jnp.float32, precision=precision
    )


def column_of(row):
    parts = []
    for k in range(row.shape[1] // 128):
        block = jnp.broadcast_to(row[:, k * 128 : (k + 1) * 128], (128, 128))
        parts.append(block.T)
    return parts[0] if len(parts) == 1 else jnp.concatenate(parts, axis=0)


def wide(column):
    return jnp.concatenate([column, column], axis=1)


def group_sums(blocks, masks, groups):
    chans = blocks[0].shape[0]
    first = second = None
    for block, keep in zip(blocks, masks):
        one = block[:, :128] + block[:, 128:]
        sq = block * block
        two = sq[:, :128] + sq[:, 128:]
        first = one * keep if first is None else first + one * keep
        second = two * keep if second is None else second + two * keep
    ones = jnp.ones((8, 128), jnp.float32)
    size = chans // groups
    row = lax.broadcasted_iota(jnp.int32, (chans, 128), 0)
    lane = lax.broadcasted_iota(jnp.int32, (chans, 128), 1)
    row_group = jnp.zeros((chans, 128), jnp.int32)
    lane_group = jnp.zeros((chans, 128), jnp.int32)
    for g in range(1, groups):
        row_group = row_group + (row >= g * size).astype(jnp.int32)
        lane_group = lane_group + (lane >= g * size).astype(jnp.int32)
    same = ((row_group == lane_group) & (lane < chans)).astype(jnp.float32)
    sums = nt_dot(ones, first, HIGH)
    squares = nt_dot(ones, second, HIGH)
    return nn_dot(sums, same, HIGH), nn_dot(squares, same, HIGH)


def fused_kernel(
    groups,
    all_rows,
    fc_ref,
    feat_any,
    cot_any,
    n1g_any,
    n1s_any,
    n2g_any,
    n2s_any,
    cb_any,
    qkvb_any,
    ob_any,
    wq_any,
    wo_any,
    wc_any,
    mixed_ref,
    grad_ref,
    feat_in,
    cot_in,
    n1g_in,
    n1s_in,
    n2g_in,
    n2s_in,
    cb_in,
    qkvb_in,
    ob_in,
    rows_ref,
    feat_ref,
    wq_ref,
    wo_ref,
    wc_ref,
    wqt_ref,
    wot_ref,
    wct_ref,
    qkvb_col,
    ob_col,
    cb_col,
    stat_ref,
    raw_ref,
    nrm_ref,
    qkv_ref,
    upd_s,
    upd_r,
    stat2_ref,
    halo_s,
    halo_r,
    hid_ref,
    stack_ref,
    cot_all,
    conv_s,
    conv_r,
    gate_s,
    gate_r,
    taps_ref,
    acc_ref,
    sum_s,
    sum_r,
    res_ref,
    send_sem,
    recv_sem,
    local_sem,
):
    frames, chans, span = feat_ref.shape
    nch = 4
    full = nch * chans
    z = lax.axis_index("ch")
    x = lax.axis_index("ha")
    d = lax.axis_index("dp")
    core = lax.rem(d, 2)
    yy = lax.div(d, 2)
    core_peer = {"dp": d + 1 - 2 * core}
    y_peer = {"dp": lax.rem(d + 2, 4)}
    x_peer = {"ha": 1 - x}
    count_f = fc_ref[0]
    masks = [jnp.where(f < count_f, 1.0, 0.0).astype(jnp.float32) for f in range(frames)]

    counter = [0]
    pending = []

    def copy_to(src, dst, dev, start=True):
        k = counter[0]
        counter[0] += 1
        c = pltpu.make_async_remote_copy(
            src_ref=src,
            dst_ref=dst,
            send_sem=send_sem.at[k],
            recv_sem=recv_sem.at[k],
            device_id=dev,
            device_id_type=MESH,
        )
        if start:
            c.start()
            pending.append(c)
        return c, k

    def arrived(dst, k):
        pltpu.make_async_remote_copy(
            src_ref=dst,
            dst_ref=dst,
            send_sem=send_sem.at[k],
            recv_sem=recv_sem.at[k],
            device_id=x_peer,
            device_id_type=MESH,
        ).wait_recv()

    loads = {}
    for k, (name, a, b) in enumerate(
        (
            ("feat", feat_any, feat_in),
            ("n1g", n1g_any, n1g_in),
            ("n1s", n1s_any, n1s_in),
            ("qkvb", qkvb_any, qkvb_in),
            ("ob", ob_any, ob_in),
            ("wq", wq_any, wq_ref),
            ("cot", cot_any, cot_in),
            ("wo", wo_any, wo_ref),
            ("wc", wc_any, wc_ref),
            ("n2g", n2g_any, n2g_in),
            ("n2s", n2s_any, n2s_in),
            ("cb", cb_any, cb_in),
        )
    ):
        loads[name] = pltpu.make_async_copy(a, b, local_sem.at[k])

    loads["feat"].start()

    barrier = pltpu.get_barrier_semaphore()
    ahead = [lax.rem(z + j, nch) for j in range(nch)]
    behind = [lax.rem(z + nch - j, nch) for j in range(nch)]
    diag_peer = {"dp": 3 - d}
    partners = [core_peer, y_peer, x_peer, diag_peer]
    for j in range(1, nch):
        partners.append({"ch": ahead[j]})
        partners.append({"ch": ahead[j], "ha": 1 - x})
    for dev in partners:
        pl.semaphore_signal(barrier, inc=1, device_id=dev, device_id_type=MESH)

    for name in loads:
        if name != "feat" and name != "wc":
            loads[name].start()

    def row_block(f, r):
        return rows_ref[pl.ds(f * 2 + r, chans, stride=2 * frames), :]

    loads["feat"].wait()
    rows_ref[...] = feat_in[...].astype(jnp.float32)
    for f in range(frames):
        for r in range(2):
            feat_ref[f, :, r * 128 : (r + 1) * 128] = row_block(f, r).astype(jnp.bfloat16)

    pl.semaphore_wait(barrier, len(partners))

    feat_k = {}
    for j in range(1, nch):
        _, feat_k[j] = copy_to(feat_ref.at[ahead[j]], raw_ref.at[0, z], {"ch": ahead[j]})
    _, feat_own_k = copy_to(feat_ref.at[z], raw_ref.at[1, z], x_peer)

    loads["wc"].start()

    first, second = group_sums(
        [feat_ref[f].astype(jnp.float32) for f in range(frames)], masks, groups
    )
    loads["n1g"].wait()
    loads["n1s"].wait()
    lanes_pad = jnp.zeros((1, 128 - chans), jnp.float32)
    own = stat_ref.at[0, z]
    own[...] = jnp.zeros((8, 128), jnp.float32)
    own[0:1, :] = first[0:1, :]
    own[1:2, :] = second[0:1, :]
    own[2:3, :] = jnp.concatenate([n1g_in[...].reshape(1, chans), lanes_pad], axis=1)
    own[3:4, :] = jnp.concatenate([n1s_in[...].reshape(1, chans), lanes_pad], axis=1)

    stat_k = []
    for j in range(nch):
        if j:
            _, k = copy_to(stat_ref.at[0, z], stat_ref.at[0, z], {"ch": ahead[j]})
            stat_k.append((0, j, k))
        _, k = copy_to(stat_ref.at[0, z], stat_ref.at[1, z], {"ch": ahead[j], "ha": 1 - x})
        stat_k.append((1, j, k))
    raw_ref[0, z] = feat_ref[z]

    line_k = {}
    shards = []

    def shard(slot, c):
        return cot_all.at[slot, pl.ds(pl.multiple_of(c * chans, chans), chans)]

    def line_step(step):
        hop = min(step, STRAIGHT)
        low, high = z - step + hop, z + step - hop
        to_up, to_down = {"ch": lax.rem(z + hop, nch)}, {"ch": lax.rem(z + nch - hop, nch)}
        up, ku = copy_to(shard(0, low), shard(0, low), to_up, start=False)
        down, kd = copy_to(shard(0, high), shard(0, high), to_down, start=False)
        up_valid = (low >= 0) & (z + hop < nch)
        down_valid = (high < nch) & (z >= hop)
        line_k[step] = (up, ku, down, kd, up_valid, down_valid)

        @pl.when(up_valid)
        def _():
            up.start()

        @pl.when(down_valid)
        def _():
            down.start()

    def spread(c, k, valid):
        on_y, ky = copy_to(shard(0, c), shard(2, c), y_peer, start=False)
        on_core, kc = copy_to(shard(0, c), shard(1, c), core_peer, start=False)
        on_far, kf = copy_to(shard(2, c), shard(3, c), core_peer, start=False)
        shards.append((c, valid, on_y, ky, on_core, kc, on_far, kf))

        @pl.when(valid)
        def _():
            if k is not None:
                arrived(shard(0, c), k)
            on_y.start()
            on_core.start()

    def line_wait(step):
        _, ku, _, kd, _, _ = line_k[step]
        spread(z - step, ku, z - step >= 0)
        spread(z + step, kd, z + step < nch)

    def pass_on(n):
        c, valid, _, ky, _, _, on_far, _ = shards[n]

        @pl.when(valid)
        def _():
            arrived(shard(2, c), ky)
            on_far.start()

    def gathered(slot):
        for c, valid, _, _, _, kc, _, kf in shards:

            @pl.when(valid)
            def _(c=c, k=kc if slot == 1 else kf):
                arrived(shard(slot, c), k)

    def line_finish(step):
        up, _, down, _, up_valid, down_valid = line_k[step]

        @pl.when(up_valid)
        def _():
            up.wait_send()

        @pl.when(down_valid)
        def _():
            down.wait_send()

    def shards_finish():
        for _, valid, on_y, _, on_core, _, on_far, _ in shards:

            @pl.when(valid)
            def _(on_y=on_y, on_core=on_core, on_far=on_far):
                on_y.wait_send()
                on_core.wait_send()
                on_far.wait_send()

    loads["cot"].wait()
    own_rows = pl.ds(pl.multiple_of(z * chans, chans), chans)
    rows_ref[...] = cot_in[...].astype(jnp.float32)
    for f in range(frames):
        for r in range(2):
            at = f * span + r * 128
            cot_all[0, own_rows, at : at + 128] = (row_block(f, r) * masks[f]).astype(jnp.bfloat16)
    spread(z, None, z >= 0)
    line_step(1)
    for name in ("qkvb", "ob", "cb", "n2g", "n2s"):
        loads[name].wait()
    qkvb_col[...] = column_of(qkvb_in[...].reshape(1, 3 * full))
    ob_col[...] = column_of(ob_in[...].reshape(1, full))
    cb_row = cb_in[...].reshape(1, chans)
    cb_col[...] = column_of(jnp.concatenate([cb_row, lanes_pad], axis=1))[:chans]
    stack_ref[:, 0 : 2 * span] = jnp.zeros((9 * chans, 2 * span), jnp.bfloat16)
    size = chans // 4
    for slot in range(4):
        taps_ref[slot, :, 0 : 2 * span] = jnp.zeros((9 * size, 2 * span), jnp.bfloat16)
    fwd_k = {}
    for j in range(1, nch):
        zs = behind[j]
        arrived(raw_ref.at[0, zs], feat_k[j])
        _, fwd_k[j] = copy_to(raw_ref.at[0, zs], raw_ref.at[1, zs], x_peer)

    loads["wq"].wait()
    loads["wo"].wait()
    for k in range(9):
        wqt_ref[k * 128 : (k + 1) * 128, :] = wq_ref[:, k * 128 : (k + 1) * 128].T
    for k in range(3):
        wot_ref[k * 128 : (k + 1) * 128, :] = wo_ref[:, k * 128 : (k + 1) * 128].T


    line_wait(1)
    line_step(2)
    for side, j, k in stat_k:
        arrived(stat_ref.at[side, behind[j]], k)
    entries = count_f.astype(jnp.float32) * float(chans // groups * all_rows * 128)

    def norm_columns(total, total_sq, gain, shift):
        mean = total / entries
        var = total_sq / entries - mean * mean
        scale = lax.rsqrt(var + EPS) * gain
        return [wide(column_of(v)[:chans]) for v in (mean, scale, shift)]

    cols = []
    for c in range(nch):
        both = stat_ref[0, c] + stat_ref[1, c]
        cols.append(
            norm_columns(both[0:1], both[1:2], stat_ref[0, c, 2:3], stat_ref[0, c, 3:4])
        )

    def normalize_side(side):
        for c in range(nch):
            mean, scale, shift = cols[c]
            block = raw_ref[side, c].astype(jnp.float32)
            nrm_ref[c * chans : (c + 1) * chans, side * span : (side + 1) * span] = (
                (block - mean) * scale + shift
            ).astype(jnp.bfloat16)

    normalize_side(0)
    bias = wide(qkvb_col[...])
    qkv_ref[:, 0:span] = (nn_dot(wqt_ref[...], nrm_ref[:, 0:span]) + bias).astype(jnp.bfloat16)
    arrived(raw_ref.at[1, z], feat_own_k)
    for j in range(1, nch):
        arrived(raw_ref.at[1, behind[j]], fwd_k[j])
    normalize_side(1)
    qkv_ref[full:, span:] = (
        nn_dot(wqt_ref[full:, :], nrm_ref[:, span:]) + bias[full:]
    ).astype(jnp.bfloat16)

    keys = qkv_ref[full : 2 * full, :].T
    scores = nn_dot(keys, qkv_ref[0:full, 0:span]) * (full ** (-0.5))
    top = jnp.max(scores, axis=0, keepdims=True)
    weights = jnp.exp(scores - top)
    total = jnp.sum(weights, axis=0, keepdims=True)
    attended = nn_dot(qkv_ref[2 * full :, :], weights.astype(jnp.bfloat16)) / total
    update = nn_dot(wot_ref[...], attended.astype(jnp.bfloat16)) + wide(ob_col[...])
    update = update.astype(jnp.bfloat16)
    for c in range(nch):
        upd_s[c] = update[c * chans : (c + 1) * chans]
    upd_k = {}
    for j in range(1, nch):
        _, upd_k[j] = copy_to(upd_s.at[ahead[j]], upd_r.at[z], {"ch": ahead[j]})
    upd_r[z] = upd_s[z]
    line_wait(2)
    line_step(3)
    pass_on(0)

    loads["wc"].wait()
    for k in range(0, TAPS * chans, 128):
        stop = min(k + 128, TAPS * chans)
        wct_ref[:, k:stop] = wc_ref[k:stop, :].T

    for j in range(1, nch):
        arrived(upd_r.at[behind[j]], upd_k[j])

    hidden = []
    for f in range(frames):
        h = (feat_ref[f].astype(jnp.float32) + upd_r[f].astype(jnp.float32)).astype(jnp.bfloat16)
        hid_ref[f] = h
        hidden.append(h.astype(jnp.float32))
        halo_s[f] = jnp.where(x == 0, h[:, 128:], h[:, :128])
    _, halo_k = copy_to(halo_s, halo_r, x_peer)
    first, second = group_sums(hidden, masks, groups)
    stat2_ref[0] = jnp.zeros((8, 128), jnp.float32)
    stat2_ref[0, 0:1, :] = first[0:1, :]
    stat2_ref[0, 1:2, :] = second[0:1, :]
    _, stat2_k = copy_to(stat2_ref.at[0], stat2_ref.at[1], x_peer)
    arrived(stat2_ref.at[1], stat2_k)
    both = stat2_ref[0] + stat2_ref[1]
    gain2 = jnp.concatenate([n2g_in[...].reshape(1, chans), lanes_pad], axis=1)
    shift2 = jnp.concatenate([n2s_in[...].reshape(1, chans), lanes_pad], axis=1)
    mean2, scale2, shift2 = norm_columns(both[0:1], both[1:2], gain2, shift2)
    mean2, scale2, shift2 = mean2[:, :128], scale2[:, :128], shift2[:, :128]
    lane = lax.broadcasted_iota(jnp.int32, (chans, 128), 1)

    def place(f, row, values):
        left = jnp.where(lane == 0, 0.0, pltpu.roll(values, 1, 1)).astype(jnp.bfloat16)
        right = jnp.where(lane == 127, 0.0, pltpu.roll(values, 127, 1)).astype(jnp.bfloat16)
        centre = values.astype(jnp.bfloat16)
        for row_tap in range(3):
            out_row = row + 1 - row_tap
            if out_row < 0 or out_row > 1:
                continue
            at = (f + 2) * span + out_row * 128
            for col_tap, v in enumerate((left, centre, right)):
                tap = row_tap * 3 + col_tap
                stack_ref[tap * chans : (tap + 1) * chans, at : at + 128] = v

    part = chans // 4
    half_frames = frames // 2

    def slice_at(f, block):
        at = (f % half_frames * 3 + block) * 128
        return f // half_frames * part, at

    def keep_slices(f, block, values):
        row, at = slice_at(f, block)
        for g in range(4):
            gate_s[g, row : row + part, at : at + 128] = values[g * part : (g + 1) * part].astype(
                jnp.bfloat16
            )

    def gate(values):
        u = (values - mean2) * scale2 + shift2
        return u / (1.0 + jnp.exp(-u))

    for f in range(frames):
        for r in range(2):
            values = gate(hid_ref[f, :, r * 128 : (r + 1) * 128].astype(jnp.float32))
            keep_slices(f, r, values)
            place(f, r, values)
    line_wait(3)
    arrived(halo_r, halo_k)
    for f in range(frames):
        values = gate(halo_r[f].astype(jnp.float32))
        keep_slices(f, 2, values)
        place(f, -1, jnp.where(x == 1, values, 0.0))
        place(f, 2, jnp.where(x == 0, values, 0.0))
    gate_k = []
    for slot, dev, g in ((1, core_peer, d + 1 - 2 * core), (2, y_peer, lax.rem(d + 2, 4)), (3, diag_peer, 3 - d)):
        _, k = copy_to(gate_s.at[g], gate_r.at[slot], dev)
        gate_k.append((slot, k))
    gate_r[0] = gate_s[d]


    conv_k = {}

    def conv_frame(f):
        acc = None
        for kt in range(3):
            term = nn_dot(
                wct_ref[:, kt * 9 * chans : (kt + 1) * 9 * chans],
                stack_ref[:, (f + kt) * span : (f + kt + 1) * span],
            )
            acc = term if acc is None else acc + term
        acc = acc.astype(jnp.bfloat16)
        for c in range(nch):
            conv_s[f, c] = acc[c * chans : (c + 1) * chans]
        for j in range(1, nch):
            _, conv_k[f, j] = copy_to(
                conv_s.at[f, ahead[j]], conv_r.at[f, z], {"ch": ahead[j]}
            )

    for f in range(CONV_FIRST):
        conv_frame(f)
    for slot, k in gate_k:
        arrived(gate_r.at[slot], k)
    lane = lax.broadcasted_iota(jnp.int32, (part, 128), 1)
    for slot in range(4):
        for f in range(frames):
            for block in range(3):
                row, at = slice_at(f, block)
                values = gate_r[slot, row : row + part, at : at + 128].astype(jnp.float32)
                windows = (
                    jnp.where(lane == 0, 0.0, pltpu.roll(values, 1, 1)),
                    values,
                    jnp.where(lane == 127, 0.0, pltpu.roll(values, 127, 1)),
                )
                if block < 2:
                    spots = [(block, windows)]
                else:
                    spots = [
                        (-1, [jnp.where(x == 1, v, 0.0) for v in windows]),
                        (2, [jnp.where(x == 0, v, 0.0) for v in windows]),
                    ]
                for row, three in spots:
                    three = [v.astype(jnp.bfloat16) for v in three]
                    for row_tap in range(3):
                        out_row = row + 1 - row_tap
                        if out_row < 0 or out_row > 1:
                            continue
                        at = (f + 2) * span + out_row * 128
                        for col_tap in range(3):
                            tap = row_tap * 3 + col_tap
                            taps_ref[slot, tap * part : (tap + 1) * part, at : at + 128] = three[
                                col_tap
                            ]

    acc_ref[TAPS * part :, :] = jnp.zeros((part, full), jnp.float32)

    def grad_taps(kt, slots):
        value = None
        for slot in slots:
            term = nt_dot(
                taps_ref[slot, :, kt * span : (kt + frames) * span], cot_all[slot]
            )
            value = term if value is None else value + term
        rows = slice(9 * part * kt, 9 * part * (kt + 1))
        acc_ref[rows, :] = value if slots[0] == 0 else acc_ref[rows, :] + value

    def rows_at(c, side):
        first, taps = RUNS[c]
        count = taps // 2 * part
        return pl.ds(pl.multiple_of(first * part + side * count, count), count)

    def run_rows(c):
        first, taps = RUNS[c]
        return slice(first * part, (first + taps) * part)

    run_k = [dict() for _ in RUNS]

    def sum_send(c):
        count = RUNS[c][1] // 2 * part
        sum_s[c, 0:count] = acc_ref[rows_at(c, 1 - x), :].astype(jnp.bfloat16)
        _, run_k[c]["sum"] = copy_to(sum_s.at[c, 0:count], sum_r.at[c, 0:count], x_peer)

    def piece(c, g, side):
        return res_ref.at[g, rows_at(c, side)]

    g_core, g_y, g_far = d + 1 - 2 * core, lax.rem(d + 2, 4), 3 - d

    def deliver(c, g):
        first, taps = RUNS[c]
        for t in range(first, min(first + taps, TAPS)):
            grad_ref[t, pl.ds(pl.multiple_of(g * part, 8), part), :] = res_ref[
                g, t * part : (t + 1) * part, :
            ].astype(jnp.float32)

    def sum_done(c):
        count = RUNS[c][1] // 2 * part
        arrived(sum_r.at[c, 0:count], run_k[c]["sum"])
        total = acc_ref[rows_at(c, x), :] + sum_r[c, 0:count].astype(jnp.float32)
        res_ref[d, rows_at(c, x), :] = total.astype(jnp.bfloat16)
        own = piece(c, d, x)
        _, run_k[c]["x"] = copy_to(own, own, x_peer)
        _, run_k[c]["y0"] = copy_to(own, own, y_peer)
        _, run_k[c]["core0"] = copy_to(own, own, core_peer)

    def pass_x(c):
        if c in Y_FIRST:
            other = piece(c, g_y, x)
            arrived(other, run_k[c]["y0"])
            _, run_k[c]["y1"] = copy_to(other, other, x_peer)
            _, run_k[c]["far"] = copy_to(other, other, core_peer)
            return
        other = piece(c, d, 1 - x)
        arrived(other, run_k[c]["x"])
        _, run_k[c]["y1"] = copy_to(other, other, y_peer)
        _, run_k[c]["core1"] = copy_to(other, other, core_peer)
        deliver(c, d)

    def pass_y(c):
        if c in Y_FIRST:
            near, away = piece(c, d, 1 - x), piece(c, g_y, 1 - x)
            arrived(near, run_k[c]["x"])
            _, run_k[c]["core1"] = copy_to(near, near, core_peer)
            arrived(away, run_k[c]["y1"])
            _, run_k[c]["far1"] = copy_to(away, away, core_peer)
            deliver(c, d)
            deliver(c, g_y)
            return
        arrived(piece(c, g_y, x), run_k[c]["y0"])
        arrived(piece(c, g_y, 1 - x), run_k[c]["y1"])
        whole = res_ref.at[g_y, run_rows(c)]
        _, run_k[c]["far"] = copy_to(whole, whole, core_peer)
        deliver(c, g_y)

    def finish(c):
        arrived(piece(c, g_core, x), run_k[c]["core0"])
        arrived(piece(c, g_core, 1 - x), run_k[c]["core1"])
        deliver(c, g_core)
        if c in Y_FIRST:
            arrived(piece(c, g_far, x), run_k[c]["far"])
            arrived(piece(c, g_far, 1 - x), run_k[c]["far1"])
        else:
            arrived(res_ref.at[g_far, run_rows(c)], run_k[c]["far"])
        deliver(c, g_far)

    gathered(1)
    grad_taps(0, (0, 1))
    for n in range(1, 7):
        pass_on(n)
    grad_taps(0, (2,))
    grad_taps(1, (0, 1, 2))
    gathered(3)
    grad_taps(0, (3,))
    sum_send(0)
    grad_taps(1, (3,))
    sum_send(1)
    grad_taps(2, (0, 1, 2, 3))
    sum_send(2)
    sum_send(3)
    sum_done(0)
    if CONV_FIRST < frames:
        conv_frame(CONV_FIRST)
    sum_done(1)
    pass_x(0)
    for f in range(CONV_FIRST + 1, frames):
        conv_frame(f)
    sum_done(2)
    pass_x(1)
    sum_done(3)
    pass_y(0)
    pass_x(2)
    pass_y(1)
    pass_x(3)
    finish(0)
    pass_y(2)
    finish(1)
    pass_y(3)
    finish(2)
    conv_bias = wide(cb_col[...])
    for f in range(frames):
        total = hid_ref[f].astype(jnp.float32) + conv_bias
        for j in range(1, nch):
            arrived(conv_r.at[f, behind[j]], conv_k[f, j])
        total = total + conv_s[f, z].astype(jnp.float32)
        for j in range(1, nch):
            total = total + conv_r[f, behind[j]].astype(jnp.float32)
        total = total * masks[f]
        for r in range(2):
            rows_ref[pl.ds(f * 2 + r, chans, stride=2 * frames), :] = total[
                :, r * 128 : (r + 1) * 128
            ]
    mixed_ref[...] = rows_ref[...].astype(jnp.bfloat16)
    finish(3)

    for c in pending:
        c.wait_send()
    shards_finish()
    for step in line_k:
        line_finish(step)


def fused_body(
    features,
    frame_count,
    norm1_gain,
    norm1_shift,
    qkv_weight,
    qkv_bias,
    out_weight,
    out_bias,
    norm2_gain,
    norm2_shift,
    conv_weight,
    conv_bias,
    cotangent,
):
    chans, clips, frames, rows, cols = features.shape
    nch = lax.axis_size("ch")
    full = nch * chans
    span = rows * cols
    groups = GROUPS // nch

    bf16, f32 = jnp.bfloat16, jnp.float32
    vm = pltpu.VMEM
    vmem = pl.BlockSpec(memory_space=pltpu.VMEM)
    hbm = pl.BlockSpec(memory_space=pltpu.HBM)
    lines = (chans * frames * rows, cols)
    scratch = [
        vm(lines, bf16),
        vm(lines, bf16),
        vm((chans,), f32),
        vm((chans,), f32),
        vm((chans,), f32),
        vm((chans,), f32),
        vm((chans,), f32),
        vm((3 * full,), f32),
        vm((full,), f32),
        vm(lines, f32),
        vm((frames, chans, span), bf16),
        vm((full, 3 * full), bf16),
        vm((full, full), bf16),
        vm((TAPS * chans, full), bf16),
        vm((3 * full, full), bf16),
        vm((full, full), bf16),
        vm((full, TAPS * chans), bf16),
        vm((3 * full, 128), f32),
        vm((full, 128), f32),
        vm((chans, 128), f32),
        vm((2, nch, 8, 128), f32),
        vm((2, nch, chans, span), bf16),
        vm((full, 2 * span), bf16),
        vm((3 * full, 2 * span), bf16),
        vm((nch, chans, span), bf16),
        vm((nch, chans, span), bf16),
        vm((2, 8, 128), f32),
        vm((frames, chans, 128), bf16),
        vm((frames, chans, 128), bf16),
        vm((frames, chans, span), bf16),
        vm((9 * chans, (frames + 2) * span), bf16),
        vm((4, full, frames * span), bf16),
        vm((frames, nch, chans, span), bf16),
        vm((frames, nch, chans, span), bf16),
        vm((4, chans // 2, frames // 2 * 3 * cols), bf16),
        vm((4, chans // 2, frames // 2 * 3 * cols), bf16),
        vm((4, 9 * (chans // 4), (frames + 2) * span), bf16),
        vm(((TAPS + 1) * (chans // 4), full), f32),
        vm((len(RUNS), chans, full), bf16),
        vm((len(RUNS), chans, full), bf16),
        vm((4, (TAPS + 1) * (chans // 4), full), bf16),
        pltpu.SemaphoreType.DMA((SEMS,)),
        pltpu.SemaphoreType.DMA((SEMS,)),
        pltpu.SemaphoreType.DMA((12,)),
    ]
    operands = (
        features.reshape(lines),
        cotangent.reshape(lines),
        norm1_gain,
        norm1_shift,
        norm2_gain,
        norm2_shift,
        conv_bias,
        qkv_bias,
        out_bias,
        qkv_weight,
        out_weight,
        conv_weight.reshape(TAPS * chans, full),
    )
    mixed, grad = pl.pallas_call(
        functools.partial(fused_kernel, groups, rows * lax.axis_size("ha")),
        out_shape=(
            jax.ShapeDtypeStruct(lines, bf16),
            jax.ShapeDtypeStruct((TAPS, chans, full), f32),
        ),
        in_specs=[pl.BlockSpec(memory_space=pltpu.SMEM)] + [hbm] * 12,
        out_specs=(vmem, vmem),
        scratch_shapes=scratch,
        compiler_params=pltpu.CompilerParams(
            collective_id=0, has_side_effects=True, vmem_limit_bytes=40 * 1024 * 1024
        ),
    )(
        frame_count,
        *(pltpu.with_memory_space_constraint(v, pltpu.HBM) for v in operands),
    )
    mixed = mixed.reshape(chans, clips, frames, rows, cols)
    grad = grad.reshape(3, 3, 3, chans, full)
    return mixed, grad


def solution(mesh):
    placed = (
        P("ch", "dp", None, "ha", None),
        P("dp"),
        P("ch"),
        P("ch"),
        P(),
        P(),
        P(),
        P(),
        P("ch"),
        P("ch"),
        P(None, None, None, "ch", None),
        P("ch"),
        P("ch", "dp", None, "ha", None),
    )
    return jax.shard_map(
        fused_body if fits_fused(mesh) else body,
        mesh=mesh,
        in_specs=placed,
        out_specs=(P("ch", "dp", None, "ha", None), P(None, None, None, "ch", None)),
        check_vma=False,
    )
```

```python
import functools

import jax
import jax.numpy as jnp
from jax import lax
from jax.experimental import pallas as pl
from jax.experimental.pallas import tpu as pltpu
from jax.sharding import PartitionSpec as P

GROUPS = 32


EPS = 1e-06


def padded_2(x, sides, width):
    for axis, dim in sides:
        count, length = (lax.axis_size(axis), x.shape[dim])
        up = [(i, (i + 1) % count) for i in range(count - 1)]
        down = [(j, i) for i, j in up]
        last = lax.slice_in_dim(x, length - width, length, axis=dim)
        leading = lax.slice_in_dim(x, 0, width, axis=dim)
        before = lax.ppermute(last, axis, up)
        after = lax.ppermute(leading, axis, down)
        x = jnp.concatenate([before, x, after], axis=dim)
    return x


def frame_mask(frame_count, frames):
    position = lax.broadcasted_iota(jnp.int32, (frame_count.shape[0], frames), 1)
    return (position < frame_count[:, None]).astype(jnp.float32)


def moments(values, mask, groups):
    chans, clips, frames, rows, cols = values.shape
    data = values.astype(jnp.float32).reshape(groups, chans // groups, clips, frames, rows * cols)
    first = jnp.einsum("gkbfp,bf->gb", data, mask)
    second = jnp.einsum("gkbfp,bf->gb", data * data, mask)
    return (first, second)


def normalize(values, first, second, count, gain, shift, groups):
    chans, clips, frames, rows, cols = values.shape
    mean = first / count[None, :]
    var = second / count[None, :] - mean * mean
    scale = lax.rsqrt(var + EPS)
    data = values.astype(jnp.float32).reshape(groups, chans // groups, clips, frames, rows * cols)
    normed = (data - mean[:, None, :, None, None]) * scale[:, None, :, None, None]
    normed = normed.reshape(values.shape)
    return normed * gain[:, None, None, None, None] + shift[:, None, None, None, None]


def attend(carry, queries, keys, values, scale):
    top, total, acc = carry
    scores = jnp.einsum("itc,isc->its", queries, keys, preferred_element_type=jnp.float32) * scale
    new_top = jnp.max(scores, axis=2)
    factor = jnp.exp(top - new_top)
    weights = jnp.exp(scores - new_top[..., None])
    total = total * factor + jnp.sum(weights, axis=2)
    acc = acc * factor[..., None] + jnp.einsum(
        "its,isc->itc", weights.astype(jnp.bfloat16), values, preferred_element_type=jnp.float32
    )
    return (new_top, total, acc)


def tap_stack(padded, time_tap, frames, rows, cols):
    windows = []
    for row_tap in range(3):
        for col_tap in range(3):
            windows.append(
                padded[
                    :,
                    :,
                    time_tap : time_tap + frames,
                    row_tap : row_tap + rows,
                    col_tap : col_tap + cols,
                ]
            )
    return jnp.concatenate(windows, axis=0)


def butterfly_sum(table, axes):
    steps = []
    for axis in axes:
        size = lax.axis_size(axis)
        for bit in range(size.bit_length() - 1):
            steps.append((axis, bit, size))
    length = table.shape[0]
    unit = (1 << len(steps)) * 8
    padded = -(-length // unit) * unit
    work = jnp.pad(table, ((0, padded - length), (0, 0)))
    for axis, bit, size in steps:
        side = (lax.axis_index(axis) >> bit) & 1
        halves = work.reshape(2, work.shape[0] // 2, work.shape[1])
        keep = lax.dynamic_index_in_dim(halves, side, keepdims=False)
        send = lax.dynamic_index_in_dim(halves, 1 - side, keepdims=False)
        perm = [(i, i ^ (1 << bit)) for i in range(size)]
        got = lax.ppermute(send.astype(jnp.bfloat16), axis, perm)
        work = keep + got.astype(jnp.float32)
    work = work.astype(jnp.bfloat16)
    for axis, bit, size in reversed(steps):
        side = (lax.axis_index(axis) >> bit) & 1
        perm = [(i, i ^ (1 << bit)) for i in range(size)]
        got = lax.ppermute(work, axis, perm)
        pair = jnp.stack([work, got])
        first = lax.dynamic_index_in_dim(pair, side, keepdims=False)
        second = lax.dynamic_index_in_dim(pair, 1 - side, keepdims=False)
        work = jnp.concatenate([first, second], axis=0)
    return work[:length].astype(jnp.float32)


def doubling_sum(values, axis):
    size = lax.axis_size(axis)
    for bit in range(size.bit_length() - 1):
        perm = [(i, i ^ (1 << bit)) for i in range(size)]
        got = lax.ppermute(values, axis, perm)
        values = tuple(a + b for a, b in zip(values, got))
    return values


def body(
    features,
    frame_count,
    norm1_gain,
    norm1_shift,
    qkv_weight,
    qkv_bias,
    out_weight,
    out_bias,
    norm2_gain,
    norm2_shift,
    conv_weight,
    conv_bias,
    cotangent,
):
    chans, clips, frames, rows, cols = features.shape
    groups = GROUPS // lax.axis_size("ch")
    mask = frame_mask(frame_count, frames)
    count = frame_count.astype(jnp.float32) * (chans // groups * rows * lax.axis_size("ha") * cols)
    first, second = moments(features, mask, groups)
    first, second = doubling_sum((first, second), "ha")
    normed = normalize(features, first, second, count, norm1_gain, norm1_shift, groups).astype(
        jnp.bfloat16
    )
    by_frame = lax.all_to_all(normed, "ch", split_axis=2, concat_axis=0, tiled=True)
    width = by_frame.shape[0]
    items = clips * by_frame.shape[2]
    tok_rows = rows * cols
    tokens = by_frame.reshape(width, items, tok_rows)
    queries = lax.dot_general(
        tokens, qkv_weight[:, :width], (((0,), (0,)), ((), ())), preferred_element_type=jnp.float32
    )
    queries = (queries + qkv_bias[:width]).astype(jnp.bfloat16)
    scale = width ** (-0.5)
    start_carry = (
        jnp.full((items, tok_rows), -jnp.inf, jnp.float32),
        jnp.zeros((items, tok_rows), jnp.float32),
        jnp.zeros((items, tok_rows, width), jnp.float32),
    )
    pairs = lax.dot_general(
        tokens, qkv_weight[:, width:], (((0,), (0,)), ((), ())), preferred_element_type=jnp.float32
    )
    pairs = (pairs + qkv_bias[width:]).astype(jnp.bfloat16)
    piece = lax.all_gather(pairs, "ha", axis=1, tiled=True)
    top, total, acc = attend(start_carry, queries, piece[..., :width], piece[..., width:], scale)
    attended = (acc / total[..., None]).astype(jnp.bfloat16)
    projected = lax.dot_general(
        out_weight, attended, (((0,), (2,)), ((), ())), preferred_element_type=jnp.float32
    )
    projected = (projected + out_bias[:, None, None]).astype(jnp.bfloat16).reshape(by_frame.shape)
    update = lax.all_to_all(projected, "ch", split_axis=0, concat_axis=2, tiled=True)
    hidden = (features.astype(jnp.float32) + update.astype(jnp.float32)).astype(jnp.bfloat16)
    first, second = moments(hidden, mask, groups)
    first, second = doubling_sum((first, second), "ha")
    gated = jax.nn.silu(
        normalize(hidden, first, second, count, norm2_gain, norm2_shift, groups)
    ).astype(jnp.bfloat16)
    with_rows = padded_2(gated, (("ha", 3),), 1)
    padded = jnp.pad(with_rows, ((0, 0), (0, 0), (2, 0), (0, 0), (1, 1)))
    stacks = [tap_stack(padded, time_tap, frames, rows, cols) for time_tap in range(3)]
    amount = chans * lax.axis_size("ch")
    summed = jnp.zeros((amount, clips, frames, rows, cols), jnp.float32)
    for time_tap in range(3):
        part = conv_weight[time_tap].reshape(9 * chans, amount)
        summed = summed + lax.dot_general(
            part, stacks[time_tap], (((0,), (0,)), ((), ())), preferred_element_type=jnp.float32
        )
    summed, stacks = lax.optimization_barrier((summed.astype(jnp.bfloat16), stacks))
    shares = lax.axis_size("ch")
    parts = summed.reshape((shares, amount // shares) + summed.shape[1:])
    parts = lax.all_to_all(parts, "ch", split_axis=0, concat_axis=0, tiled=True)
    conv_out = jnp.sum(parts.astype(jnp.float32), axis=0)
    mixed = mask[None, :, :, None, None] * (
        hidden.astype(jnp.float32) + conv_out + conv_bias[:, None, None, None, None]
    )
    mixed = mixed.astype(jnp.bfloat16)
    masked_cot = cotangent * mask.astype(jnp.bfloat16)[None, :, :, None, None]
    full_width = chans * lax.axis_size("ch")
    carry = jnp.zeros((3, 9 * chans, full_width), jnp.float32)
    copies = jnp.broadcast_to(masked_cot[None], (shares,) + masked_cot.shape)
    piece = lax.all_to_all(copies, "ch", split_axis=0, concat_axis=0, tiled=True)
    piece = piece.reshape((shares * chans,) + masked_cot.shape[1:])
    start = jnp.int32(0)
    for time_tap in range(3):
        part = lax.dot_general(
            stacks[time_tap],
            piece,
            (((1, 2, 3, 4), (1, 2, 3, 4)), ((), ())),
            preferred_element_type=jnp.float32,
        )
        carry = lax.dynamic_update_slice(
            carry, part[None], (jnp.int32(time_tap), jnp.int32(0), start)
        )
    weight_grad = butterfly_sum(carry.reshape(27 * chans, full_width), ("dp", "ha"))
    weight_grad = weight_grad.reshape(3, 3, 3, chans, full_width)
    return (mixed, weight_grad)


MESH = pl.DeviceIdType.MESH
HIGH = lax.Precision.HIGHEST
SEMS = 128
TAPS = 27
CONV_FIRST = 2
STRAIGHT = 1
Y_FIRST = (2, 3)
RUNS = ((0, 8), (8, 8), (16, 8), (24, 4))


def fits_fused(mesh):
    return mesh.shape["ch"] == 4 and mesh.shape["ha"] == 2 and mesh.shape["dp"] == 4


def nt_dot(a, b, precision=None):
    return lax.dot_general(
        a, b, (((1,), (1,)), ((), ())), preferred_element_type=jnp.float32, precision=precision
    )


def nn_dot(a, b, precision=None):
    return lax.dot_general(
        a, b, (((1,), (0,)), ((), ())), preferred_element_type=jnp.float32, precision=precision
    )


def column_of(row):
    parts = []
    for k in range(row.shape[1] // 128):
        block = jnp.broadcast_to(row[:, k * 128 : (k + 1) * 128], (128, 128))
        parts.append(block.T)
    return parts[0] if len(parts) == 1 else jnp.concatenate(parts, axis=0)


def wide(column):
    return jnp.concatenate([column, column], axis=1)


def group_sums(blocks, masks, groups):
    chans = blocks[0].shape[0]
    first = second = None
    for block, keep in zip(blocks, masks):
        one = block[:, :128] + block[:, 128:]
        sq = block * block
        two = sq[:, :128] + sq[:, 128:]
        first = one * keep if first is None else first + one * keep
        second = two * keep if second is None else second + two * keep
    ones = jnp.ones((8, 128), jnp.float32)
    size = chans // groups
    row = lax.broadcasted_iota(jnp.int32, (chans, 128), 0)
    lane = lax.broadcasted_iota(jnp.int32, (chans, 128), 1)
    row_group = jnp.zeros((chans, 128), jnp.int32)
    lane_group = jnp.zeros((chans, 128), jnp.int32)
    for g in range(1, groups):
        row_group = row_group + (row >= g * size).astype(jnp.int32)
        lane_group = lane_group + (lane >= g * size).astype(jnp.int32)
    same = ((row_group == lane_group) & (lane < chans)).astype(jnp.float32)
    sums = nt_dot(ones, first, HIGH)
    squares = nt_dot(ones, second, HIGH)
    return nn_dot(sums, same, HIGH), nn_dot(squares, same, HIGH)


def fused_kernel(
    groups,
    all_rows,
    fc_ref,
    feat_any,
    cot_any,
    n1g_any,
    n1s_any,
    n2g_any,
    n2s_any,
    cb_any,
    qkvb_any,
    ob_any,
    wq_any,
    wo_any,
    wc_any,
    mixed_ref,
    grad_ref,
    feat_in,
    cot_in,
    n1g_in,
    n1s_in,
    n2g_in,
    n2s_in,
    cb_in,
    qkvb_in,
    ob_in,
    rows_ref,
    feat_ref,
    wq_ref,
    wo_ref,
    wc_ref,
    wqt_ref,
    wot_ref,
    wct_ref,
    qkvb_col,
    ob_col,
    cb_col,
    stat_ref,
    raw_ref,
    nrm_ref,
    qkv_ref,
    upd_s,
    upd_r,
    stat2_ref,
    halo_s,
    halo_r,
    hid_ref,
    stack_ref,
    cot_all,
    conv_s,
    conv_r,
    gate_s,
    gate_r,
    taps_ref,
    acc_ref,
    sum_s,
    sum_r,
    res_ref,
    send_sem,
    recv_sem,
    local_sem,
):
    frames, chans, span = feat_ref.shape
    nch = 4
    full = nch * chans
    z = lax.axis_index("ch")
    x = lax.axis_index("ha")
    d = lax.axis_index("dp")
    core = lax.rem(d, 2)
    yy = lax.div(d, 2)
    core_peer = {"dp": d + 1 - 2 * core}
    y_peer = {"dp": lax.rem(d + 2, 4)}
    x_peer = {"ha": 1 - x}
    count_f = fc_ref[0]
    masks = [jnp.where(f < count_f, 1.0, 0.0).astype(jnp.float32) for f in range(frames)]

    counter = [0]
    pending = []

    def copy_to(src, dst, dev, start=True):
        k = counter[0]
        counter[0] += 1
        c = pltpu.make_async_remote_copy(
            src_ref=src,
            dst_ref=dst,
            send_sem=send_sem.at[k],
            recv_sem=recv_sem.at[k],
            device_id=dev,
            device_id_type=MESH,
        )
        if start:
            c.start()
            pending.append(c)
        return c, k

    def arrived(dst, k):
        pltpu.make_async_remote_copy(
            src_ref=dst,
            dst_ref=dst,
            send_sem=send_sem.at[k],
            recv_sem=recv_sem.at[k],
            device_id=x_peer,
            device_id_type=MESH,
        ).wait_recv()

    loads = {}
    for k, (name, a, b) in enumerate(
        (
            ("feat", feat_any, feat_in),
            ("n1g", n1g_any, n1g_in),
            ("n1s", n1s_any, n1s_in),
            ("qkvb", qkvb_any, qkvb_in),
            ("ob", ob_any, ob_in),
            ("wq", wq_any, wq_ref),
            ("cot", cot_any, cot_in),
            ("wo", wo_any, wo_ref),
            ("wc", wc_any, wc_ref),
            ("n2g", n2g_any, n2g_in),
            ("n2s", n2s_any, n2s_in),
            ("cb", cb_any, cb_in),
        )
    ):
        loads[name] = pltpu.make_async_copy(a, b, local_sem.at[k])

    loads["feat"].start()

    barrier = pltpu.get_barrier_semaphore()
    ahead = [lax.rem(z + j, nch) for j in range(nch)]
    behind = [lax.rem(z + nch - j, nch) for j in range(nch)]
    diag_peer = {"dp": 3 - d}
    partners = [core_peer, y_peer, x_peer, diag_peer]
    for j in range(1, nch):
        partners.append({"ch": ahead[j]})
        partners.append({"ch": ahead[j], "ha": 1 - x})
    for dev in partners:
        pl.semaphore_signal(barrier, inc=1, device_id=dev, device_id_type=MESH)

    for name in loads:
        if name != "feat" and name != "wc":
            loads[name].start()

    def row_block(f, r):
        return rows_ref[pl.ds(f * 2 + r, chans, stride=2 * frames), :]

    loads["feat"].wait()
    rows_ref[...] = feat_in[...].astype(jnp.float32)
    for f in range(frames):
        for r in range(2):
            feat_ref[f, :, r * 128 : (r + 1) * 128] = row_block(f, r).astype(jnp.bfloat16)

    pl.semaphore_wait(barrier, len(partners))

    feat_k = {}
    for j in range(1, nch):
        _, feat_k[j] = copy_to(feat_ref.at[ahead[j]], raw_ref.at[0, z], {"ch": ahead[j]})
    _, feat_own_k = copy_to(feat_ref.at[z], raw_ref.at[1, z], x_peer)

    loads["wc"].start()

    first, second = group_sums(
        [feat_ref[f].astype(jnp.float32) for f in range(frames)], masks, groups
    )
    loads["n1g"].wait()
    loads["n1s"].wait()
    lanes_pad = jnp.zeros((1, 128 - chans), jnp.float32)
    own = stat_ref.at[0, z]
    own[...] = jnp.zeros((8, 128), jnp.float32)
    own[0:1, :] = first[0:1, :]
    own[1:2, :] = second[0:1, :]
    own[2:3, :] = jnp.concatenate([n1g_in[...].reshape(1, chans), lanes_pad], axis=1)
    own[3:4, :] = jnp.concatenate([n1s_in[...].reshape(1, chans), lanes_pad], axis=1)

    stat_k = []
    for j in range(nch):
        if j:
            _, k = copy_to(stat_ref.at[0, z], stat_ref.at[0, z], {"ch": ahead[j]})
            stat_k.append((0, j, k))
        _, k = copy_to(stat_ref.at[0, z], stat_ref.at[1, z], {"ch": ahead[j], "ha": 1 - x})
        stat_k.append((1, j, k))
    raw_ref[0, z] = feat_ref[z]

    line_k = {}
    shards = []

    def shard(slot, c):
        return cot_all.at[slot, pl.ds(pl.multiple_of(c * chans, chans), chans)]

    def line_step(step):
        hop = min(step, STRAIGHT)
        low, high = z - step + hop, z + step - hop
        to_up, to_down = {"ch": lax.rem(z + hop, nch)}, {"ch": lax.rem(z + nch - hop, nch)}
        up, ku = copy_to(shard(0, low), shard(0, low), to_up, start=False)
        down, kd = copy_to(shard(0, high), shard(0, high), to_down, start=False)
        up_valid = (low >= 0) & (z + hop < nch)
        down_valid = (high < nch) & (z >= hop)
        line_k[step] = (up, ku, down, kd, up_valid, down_valid)

        @pl.when(up_valid)
        def _():
            up.start()

        @pl.when(down_valid)
        def _():
            down.start()

    def spread(c, k, valid):
        on_y, ky = copy_to(shard(0, c), shard(2, c), y_peer, start=False)
        on_core, kc = copy_to(shard(0, c), shard(1, c), core_peer, start=False)
        on_far, kf = copy_to(shard(2, c), shard(3, c), core_peer, start=False)
        shards.append((c, valid, on_y, ky, on_core, kc, on_far, kf))

        @pl.when(valid)
        def _():
            if k is not None:
                arrived(shard(0, c), k)
            on_y.start()
            on_core.start()

    def line_wait(step):
        _, ku, _, kd, _, _ = line_k[step]
        spread(z - step, ku, z - step >= 0)
        spread(z + step, kd, z + step < nch)

    def pass_on(n):
        c, valid, _, ky, _, _, on_far, _ = shards[n]

        @pl.when(valid)
        def _():
            arrived(shard(2, c), ky)
            on_far.start()

    def gathered(slot):
        for c, valid, _, _, _, kc, _, kf in shards:

            @pl.when(valid)
            def _(c=c, k=kc if slot == 1 else kf):
                arrived(shard(slot, c), k)

    def line_finish(step):
        up, _, down, _, up_valid, down_valid = line_k[step]

        @pl.when(up_valid)
        def _():
            up.wait_send()

        @pl.when(down_valid)
        def _():
            down.wait_send()

    def shards_finish():
        for _, valid, on_y, _, on_core, _, on_far, _ in shards:

            @pl.when(valid)
            def _(on_y=on_y, on_core=on_core, on_far=on_far):
                on_y.wait_send()
                on_core.wait_send()
                on_far.wait_send()

    loads["cot"].wait()
    own_rows = pl.ds(pl.multiple_of(z * chans, chans), chans)
    rows_ref[...] = cot_in[...].astype(jnp.float32)
    for f in range(frames):
        for r in range(2):
            at = f * span + r * 128
            cot_all[0, own_rows, at : at + 128] = (row_block(f, r) * masks[f]).astype(jnp.bfloat16)
    spread(z, None, z >= 0)
    line_step(1)
    for name in ("qkvb", "ob", "cb", "n2g", "n2s"):
        loads[name].wait()
    qkvb_col[...] = column_of(qkvb_in[...].reshape(1, 3 * full))
    ob_col[...] = column_of(ob_in[...].reshape(1, full))
    cb_row = cb_in[...].reshape(1, chans)
    cb_col[...] = column_of(jnp.concatenate([cb_row, lanes_pad], axis=1))[:chans]
    stack_ref[:, 0 : 2 * span] = jnp.zeros((9 * chans, 2 * span), jnp.bfloat16)
    size = chans // 4
    for slot in range(4):
        taps_ref[slot, :, 0 : 2 * span] = jnp.zeros((9 * size, 2 * span), jnp.bfloat16)
    fwd_k = {}
    for j in range(1, nch):
        zs = behind[j]
        arrived(raw_ref.at[0, zs], feat_k[j])
        _, fwd_k[j] = copy_to(raw_ref.at[0, zs], raw_ref.at[1, zs], x_peer)

    loads["wq"].wait()
    loads["wo"].wait()
    for k in range(9):
        wqt_ref[k * 128 : (k + 1) * 128, :] = wq_ref[:, k * 128 : (k + 1) * 128].T
    for k in range(3):
        wot_ref[k * 128 : (k + 1) * 128, :] = wo_ref[:, k * 128 : (k + 1) * 128].T


    line_wait(1)
    line_step(2)
    for side, j, k in stat_k:
        arrived(stat_ref.at[side, behind[j]], k)
    entries = count_f.astype(jnp.float32) * float(chans // groups * all_rows * 128)

    def norm_columns(total, total_sq, gain, shift):
        mean = total / entries
        var = total_sq / entries - mean * mean
        scale = lax.rsqrt(var + EPS) * gain
        return [wide(column_of(v)[:chans]) for v in (mean, scale, shift)]

    cols = []
    for c in range(nch):
        both = stat_ref[0, c] + stat_ref[1, c]
        cols.append(
            norm_columns(both[0:1], both[1:2], stat_ref[0, c, 2:3], stat_ref[0, c, 3:4])
        )

    def normalize_side(side):
        for c in range(nch):
            mean, scale, shift = cols[c]
            block = raw_ref[side, c].astype(jnp.float32)
            nrm_ref[c * chans : (c + 1) * chans, side * span : (side + 1) * span] = (
                (block - mean) * scale + shift
            ).astype(jnp.bfloat16)

    normalize_side(0)
    bias = wide(qkvb_col[...])
    qkv_ref[:, 0:span] = (nn_dot(wqt_ref[...], nrm_ref[:, 0:span]) + bias).astype(jnp.bfloat16)
    arrived(raw_ref.at[1, z], feat_own_k)
    for j in range(1, nch):
        arrived(raw_ref.at[1, behind[j]], fwd_k[j])
    normalize_side(1)
    qkv_ref[full:, span:] = (
        nn_dot(wqt_ref[full:, :], nrm_ref[:, span:]) + bias[full:]
    ).astype(jnp.bfloat16)

    keys = qkv_ref[full : 2 * full, :].T
    scores = nn_dot(keys, qkv_ref[0:full, 0:span]) * (full ** (-0.5))
    top = jnp.max(scores, axis=0, keepdims=True)
    weights = jnp.exp(scores - top)
    total = jnp.sum(weights, axis=0, keepdims=True)
    attended = nn_dot(qkv_ref[2 * full :, :], weights.astype(jnp.bfloat16)) / total
    update = nn_dot(wot_ref[...], attended.astype(jnp.bfloat16)) + wide(ob_col[...])
    update = update.astype(jnp.bfloat16)
    for c in range(nch):
        upd_s[c] = update[c * chans : (c + 1) * chans]
    upd_k = {}
    for j in range(1, nch):
        _, upd_k[j] = copy_to(upd_s.at[ahead[j]], upd_r.at[z], {"ch": ahead[j]})
    upd_r[z] = upd_s[z]
    line_wait(2)
    line_step(3)
    pass_on(0)

    loads["wc"].wait()
    for k in range(0, TAPS * chans, 128):
        stop = min(k + 128, TAPS * chans)
        wct_ref[:, k:stop] = wc_ref[k:stop, :].T

    for j in range(1, nch):
        arrived(upd_r.at[behind[j]], upd_k[j])

    hidden = []
    for f in range(frames):
        h = (feat_ref[f].astype(jnp.float32) + upd_r[f].astype(jnp.float32)).astype(jnp.bfloat16)
        hid_ref[f] = h
        hidden.append(h.astype(jnp.float32))
        halo_s[f] = jnp.where(x == 0, h[:, 128:], h[:, :128])
    _, halo_k = copy_to(halo_s, halo_r, x_peer)
    first, second = group_sums(hidden, masks, groups)
    stat2_ref[0] = jnp.zeros((8, 128), jnp.float32)
    stat2_ref[0, 0:1, :] = first[0:1, :]
    stat2_ref[0, 1:2, :] = second[0:1, :]
    _, stat2_k = copy_to(stat2_ref.at[0], stat2_ref.at[1], x_peer)
    arrived(stat2_ref.at[1], stat2_k)
    both = stat2_ref[0] + stat2_ref[1]
    gain2 = jnp.concatenate([n2g_in[...].reshape(1, chans), lanes_pad], axis=1)
    shift2 = jnp.concatenate([n2s_in[...].reshape(1, chans), lanes_pad], axis=1)
    mean2, scale2, shift2 = norm_columns(both[0:1], both[1:2], gain2, shift2)
    mean2, scale2, shift2 = mean2[:, :128], scale2[:, :128], shift2[:, :128]
    lane = lax.broadcasted_iota(jnp.int32, (chans, 128), 1)

    def place(f, row, values):
        left = jnp.where(lane == 0, 0.0, pltpu.roll(values, 1, 1)).astype(jnp.bfloat16)
        right = jnp.where(lane == 127, 0.0, pltpu.roll(values, 127, 1)).astype(jnp.bfloat16)
        centre = values.astype(jnp.bfloat16)
        for row_tap in range(3):
            out_row = row + 1 - row_tap
            if out_row < 0 or out_row > 1:
                continue
            at = (f + 2) * span + out_row * 128
            for col_tap, v in enumerate((left, centre, right)):
                tap = row_tap * 3 + col_tap
                stack_ref[tap * chans : (tap + 1) * chans, at : at + 128] = v

    part = chans // 4
    half_frames = frames // 2

    def slice_at(f, block):
        at = (f % half_frames * 3 + block) * 128
        return f // half_frames * part, at

    def keep_slices(f, block, values):
        row, at = slice_at(f, block)
        for g in range(4):
            gate_s[g, row : row + part, at : at + 128] = values[g * part : (g + 1) * part].astype(
                jnp.bfloat16
            )

    def gate(values):
        u = (values - mean2) * scale2 + shift2
        return u / (1.0 + jnp.exp(-u))

    gated = []
    for f in range(frames):
        for r in range(2):
            values = gate(hid_ref[f, :, r * 128 : (r + 1) * 128].astype(jnp.float32))
            keep_slices(f, r, values)
            gated.append((f, r, values))
    line_wait(3)
    arrived(halo_r, halo_k)
    for f in range(frames):
        values = gate(halo_r[f].astype(jnp.float32))
        keep_slices(f, 2, values)
        gated.append((f, -1, jnp.where(x == 1, values, 0.0)))
        gated.append((f, 2, jnp.where(x == 0, values, 0.0)))
    gate_k = []
    for slot, dev, g in ((1, core_peer, d + 1 - 2 * core), (2, y_peer, lax.rem(d + 2, 4)), (3, diag_peer, 3 - d)):
        _, k = copy_to(gate_s.at[g], gate_r.at[slot], dev)
        gate_k.append((slot, k))
    gate_r[0] = gate_s[d]
    for f, r, values in gated:
        place(f, r, values)


    conv_k = {}

    def conv_frame(f):
        acc = None
        for kt in range(3):
            term = nn_dot(
                wct_ref[:, kt * 9 * chans : (kt + 1) * 9 * chans],
                stack_ref[:, (f + kt) * span : (f + kt + 1) * span],
            )
            acc = term if acc is None else acc + term
        acc = acc.astype(jnp.bfloat16)
        for c in range(nch):
            conv_s[f, c] = acc[c * chans : (c + 1) * chans]
        for j in range(1, nch):
            _, conv_k[f, j] = copy_to(
                conv_s.at[f, ahead[j]], conv_r.at[f, z], {"ch": ahead[j]}
            )

    for f in range(CONV_FIRST):
        conv_frame(f)
    for slot, k in gate_k:
        arrived(gate_r.at[slot], k)
    lane = lax.broadcasted_iota(jnp.int32, (part, 128), 1)
    for slot in range(4):
        for f in range(frames):
            for block in range(3):
                row, at = slice_at(f, block)
                values = gate_r[slot, row : row + part, at : at + 128].astype(jnp.float32)
                windows = (
                    jnp.where(lane == 0, 0.0, pltpu.roll(values, 1, 1)),
                    values,
                    jnp.where(lane == 127, 0.0, pltpu.roll(values, 127, 1)),
                )
                if block < 2:
                    spots = [(block, windows)]
                else:
                    spots = [
                        (-1, [jnp.where(x == 1, v, 0.0) for v in windows]),
                        (2, [jnp.where(x == 0, v, 0.0) for v in windows]),
                    ]
                for row, three in spots:
                    three = [v.astype(jnp.bfloat16) for v in three]
                    for row_tap in range(3):
                        out_row = row + 1 - row_tap
                        if out_row < 0 or out_row > 1:
                            continue
                        at = (f + 2) * span + out_row * 128
                        for col_tap in range(3):
                            tap = row_tap * 3 + col_tap
                            taps_ref[slot, tap * part : (tap + 1) * part, at : at + 128] = three[
                                col_tap
                            ]

    acc_ref[TAPS * part :, :] = jnp.zeros((part, full), jnp.float32)

    def grad_taps(kt, slots):
        value = None
        for slot in slots:
            term = nt_dot(
                taps_ref[slot, :, kt * span : (kt + frames) * span], cot_all[slot]
            )
            value = term if value is None else value + term
        rows = slice(9 * part * kt, 9 * part * (kt + 1))
        acc_ref[rows, :] = value if slots[0] == 0 else acc_ref[rows, :] + value

    def rows_at(c, side):
        first, taps = RUNS[c]
        count = taps // 2 * part
        return pl.ds(pl.multiple_of(first * part + side * count, count), count)

    def run_rows(c):
        first, taps = RUNS[c]
        return slice(first * part, (first + taps) * part)

    run_k = [dict() for _ in RUNS]

    def sum_send(c):
        count = RUNS[c][1] // 2 * part
        sum_s[c, 0:count] = acc_ref[rows_at(c, 1 - x), :].astype(jnp.bfloat16)
        _, run_k[c]["sum"] = copy_to(sum_s.at[c, 0:count], sum_r.at[c, 0:count], x_peer)

    def piece(c, g, side):
        return res_ref.at[g, rows_at(c, side)]

    g_core, g_y, g_far = d + 1 - 2 * core, lax.rem(d + 2, 4), 3 - d

    def deliver(c, g):
        first, taps = RUNS[c]
        for t in range(first, min(first + taps, TAPS)):
            grad_ref[t, pl.ds(pl.multiple_of(g * part, 8), part), :] = res_ref[
                g, t * part : (t + 1) * part, :
            ].astype(jnp.float32)

    def sum_done(c):
        count = RUNS[c][1] // 2 * part
        arrived(sum_r.at[c, 0:count], run_k[c]["sum"])
        total = acc_ref[rows_at(c, x), :] + sum_r[c, 0:count].astype(jnp.float32)
        res_ref[d, rows_at(c, x), :] = total.astype(jnp.bfloat16)
        own = piece(c, d, x)
        _, run_k[c]["x"] = copy_to(own, own, x_peer)
        _, run_k[c]["y0"] = copy_to(own, own, y_peer)
        _, run_k[c]["core0"] = copy_to(own, own, core_peer)

    def pass_x(c):
        if c in Y_FIRST:
            other = piece(c, g_y, x)
            arrived(other, run_k[c]["y0"])
            _, run_k[c]["y1"] = copy_to(other, other, x_peer)
            _, run_k[c]["far"] = copy_to(other, other, core_peer)
            return
        other = piece(c, d, 1 - x)
        arrived(other, run_k[c]["x"])
        _, run_k[c]["y1"] = copy_to(other, other, y_peer)
        _, run_k[c]["core1"] = copy_to(other, other, core_peer)
        deliver(c, d)

    def pass_y(c):
        if c in Y_FIRST:
            near, away = piece(c, d, 1 - x), piece(c, g_y, 1 - x)
            arrived(near, run_k[c]["x"])
            _, run_k[c]["core1"] = copy_to(near, near, core_peer)
            arrived(away, run_k[c]["y1"])
            _, run_k[c]["far1"] = copy_to(away, away, core_peer)
            deliver(c, d)
            deliver(c, g_y)
            return
        arrived(piece(c, g_y, x), run_k[c]["y0"])
        arrived(piece(c, g_y, 1 - x), run_k[c]["y1"])
        whole = res_ref.at[g_y, run_rows(c)]
        _, run_k[c]["far"] = copy_to(whole, whole, core_peer)
        deliver(c, g_y)

    def finish(c):
        arrived(piece(c, g_core, x), run_k[c]["core0"])
        arrived(piece(c, g_core, 1 - x), run_k[c]["core1"])
        deliver(c, g_core)
        if c in Y_FIRST:
            arrived(piece(c, g_far, x), run_k[c]["far"])
            arrived(piece(c, g_far, 1 - x), run_k[c]["far1"])
        else:
            arrived(res_ref.at[g_far, run_rows(c)], run_k[c]["far"])
        deliver(c, g_far)

    gathered(1)
    grad_taps(0, (0, 1))
    for n in range(1, 7):
        pass_on(n)
    grad_taps(0, (2,))
    grad_taps(1, (0, 1, 2))
    gathered(3)
    grad_taps(0, (3,))
    sum_send(0)
    grad_taps(1, (3,))
    sum_send(1)
    grad_taps(2, (0, 1, 2, 3))
    sum_send(2)
    sum_send(3)
    sum_done(0)
    if CONV_FIRST < frames:
        conv_frame(CONV_FIRST)
    sum_done(1)
    pass_x(0)
    for f in range(CONV_FIRST + 1, frames):
        conv_frame(f)
    sum_done(2)
    pass_x(1)
    sum_done(3)
    pass_y(0)
    pass_x(2)
    pass_y(1)
    pass_x(3)
    finish(0)
    pass_y(2)
    finish(1)
    pass_y(3)
    finish(2)
    conv_bias = wide(cb_col[...])
    for f in range(frames):
        total = hid_ref[f].astype(jnp.float32) + conv_bias
        for j in range(1, nch):
            arrived(conv_r.at[f, behind[j]], conv_k[f, j])
        total = total + conv_s[f, z].astype(jnp.float32)
        for j in range(1, nch):
            total = total + conv_r[f, behind[j]].astype(jnp.float32)
        total = total * masks[f]
        for r in range(2):
            rows_ref[pl.ds(f * 2 + r, chans, stride=2 * frames), :] = total[
                :, r * 128 : (r + 1) * 128
            ]
    mixed_ref[...] = rows_ref[...].astype(jnp.bfloat16)
    finish(3)

    for c in pending:
        c.wait_send()
    shards_finish()
    for step in line_k:
        line_finish(step)


def fused_body(
    features,
    frame_count,
    norm1_gain,
    norm1_shift,
    qkv_weight,
    qkv_bias,
    out_weight,
    out_bias,
    norm2_gain,
    norm2_shift,
    conv_weight,
    conv_bias,
    cotangent,
):
    chans, clips, frames, rows, cols = features.shape
    nch = lax.axis_size("ch")
    full = nch * chans
    span = rows * cols
    groups = GROUPS // nch

    bf16, f32 = jnp.bfloat16, jnp.float32
    vm = pltpu.VMEM
    vmem = pl.BlockSpec(memory_space=pltpu.VMEM)
    hbm = pl.BlockSpec(memory_space=pltpu.HBM)
    lines = (chans * frames * rows, cols)
    scratch = [
        vm(lines, bf16),
        vm(lines, bf16),
        vm((chans,), f32),
        vm((chans,), f32),
        vm((chans,), f32),
        vm((chans,), f32),
        vm((chans,), f32),
        vm((3 * full,), f32),
        vm((full,), f32),
        vm(lines, f32),
        vm((frames, chans, span), bf16),
        vm((full, 3 * full), bf16),
        vm((full, full), bf16),
        vm((TAPS * chans, full), bf16),
        vm((3 * full, full), bf16),
        vm((full, full), bf16),
        vm((full, TAPS * chans), bf16),
        vm((3 * full, 128), f32),
        vm((full, 128), f32),
        vm((chans, 128), f32),
        vm((2, nch, 8, 128), f32),
        vm((2, nch, chans, span), bf16),
        vm((full, 2 * span), bf16),
        vm((3 * full, 2 * span), bf16),
        vm((nch, chans, span), bf16),
        vm((nch, chans, span), bf16),
        vm((2, 8, 128), f32),
        vm((frames, chans, 128), bf16),
        vm((frames, chans, 128), bf16),
        vm((frames, chans, span), bf16),
        vm((9 * chans, (frames + 2) * span), bf16),
        vm((4, full, frames * span), bf16),
        vm((frames, nch, chans, span), bf16),
        vm((frames, nch, chans, span), bf16),
        vm((4, chans // 2, frames // 2 * 3 * cols), bf16),
        vm((4, chans // 2, frames // 2 * 3 * cols), bf16),
        vm((4, 9 * (chans // 4), (frames + 2) * span), bf16),
        vm(((TAPS + 1) * (chans // 4), full), f32),
        vm((len(RUNS), chans, full), bf16),
        vm((len(RUNS), chans, full), bf16),
        vm((4, (TAPS + 1) * (chans // 4), full), bf16),
        pltpu.SemaphoreType.DMA((SEMS,)),
        pltpu.SemaphoreType.DMA((SEMS,)),
        pltpu.SemaphoreType.DMA((12,)),
    ]
    operands = (
        features.reshape(lines),
        cotangent.reshape(lines),
        norm1_gain,
        norm1_shift,
        norm2_gain,
        norm2_shift,
        conv_bias,
        qkv_bias,
        out_bias,
        qkv_weight,
        out_weight,
        conv_weight.reshape(TAPS * chans, full),
    )
    mixed, grad = pl.pallas_call(
        functools.partial(fused_kernel, groups, rows * lax.axis_size("ha")),
        out_shape=(
            jax.ShapeDtypeStruct(lines, bf16),
            jax.ShapeDtypeStruct((TAPS, chans, full), f32),
        ),
        in_specs=[pl.BlockSpec(memory_space=pltpu.SMEM)] + [hbm] * 12,
        out_specs=(vmem, vmem),
        scratch_shapes=scratch,
        compiler_params=pltpu.CompilerParams(
            collective_id=0, has_side_effects=True, vmem_limit_bytes=40 * 1024 * 1024
        ),
    )(
        frame_count,
        *(pltpu.with_memory_space_constraint(v, pltpu.HBM) for v in operands),
    )
    mixed = mixed.reshape(chans, clips, frames, rows, cols)
    grad = grad.reshape(3, 3, 3, chans, full)
    return mixed, grad


def solution(mesh):
    placed = (
        P("ch", "dp", None, "ha", None),
        P("dp"),
        P("ch"),
        P("ch"),
        P(),
        P(),
        P(),
        P(),
        P("ch"),
        P("ch"),
        P(None, None, None, "ch", None),
        P("ch"),
        P("ch", "dp", None, "ha", None),
    )
    return jax.shard_map(
        fused_body if fits_fused(mesh) else body,
        mesh=mesh,
        in_specs=placed,
        out_specs=(P("ch", "dp", None, "ha", None), P(None, None, None, "ch", None)),
        check_vma=False,
    )
```
